128 devices in a mesh: lat: 8 (over y, core), lon: 16 (over x, z).
Axes of the slice: x: 4, y: 4, z: 4, core: 2. Of those that a mesh axis runs over, the one named last changes fastest.
Arguments:
- grid_latent: bfloat16 [262144, 512], P(('lat', 'lon')), may hold values from -6 to 6
- mesh_latent: bfloat16 [10240, 512], P(('lat', 'lon')), may hold values from -6 to 6
- encoder_slots: int32 [2, 262144], P(None, ('lat', 'lon')), may hold values from 0 to 719, as said below
- decoder_slots: int32 [3, 262144], P(None, ('lat', 'lon')), may hold values from 0 to 719, as said below
- peer_rows: int32 [128, 128, 4], P(('lat', 'lon')), may hold values from 0 to 79, as said below
- edge_source: int32 [81920], P(('lat', 'lon')), may hold values from 0 to 511
- edge_target: int32 [81920], P(('lat', 'lon')), may hold values from 0 to 79
- encoder_sender: bfloat16 [512, 512], replicated, may hold values from -0.25 to 0.25
- encoder_receiver: bfloat16 [512, 512], replicated, may hold values from -0.25 to 0.25
- encoder_output: bfloat16 [512, 512], replicated, may hold values from -0.25 to 0.25
- encoder_merge: bfloat16 [512, 512], replicated, may hold values from -0.25 to 0.25
- encoder_self: bfloat16 [512, 512], replicated, may hold values from -0.25 to 0.25
- process_sender: bfloat16 [2, 512, 512], replicated, may hold values from -0.25 to 0.25
- process_receiver: bfloat16 [2, 512, 512], replicated, may hold values from -0.25 to 0.25
- process_output: bfloat16 [2, 512, 512], replicated, may hold values from -0.25 to 0.25
- process_merge: bfloat16 [2, 512, 512], replicated, may hold values from -0.25 to 0.25
- process_self: bfloat16 [2, 512, 512], replicated, may hold values from -0.25 to 0.25
- decoder_sender: bfloat16 [512, 512], replicated, may hold values from -0.25 to 0.25
- decoder_receiver: bfloat16 [512, 512], replicated, may hold values from -0.25 to 0.25
- decoder_output: bfloat16 [512, 512], replicated, may hold values from -0.25 to 0.25
Outputs:
- grid_update: bfloat16 [262144, 512], P(('lat', 'lon'))
The draws below stay inside these ranges and needn't reach their ends.
Inputs may be any that keep to these rules, and one draw needn't show every extreme that they name: `encoder_slots`: every slot names a mesh node of the grid node's own tile or of one of its up to eight neighbouring tiles that exists in the window. `decoder_slots`: every slot names a mesh node of the grid node's own tile or of one of its up to eight neighbouring tiles that exists in the window. `peer_rows`: for each pair of tiles the 4 entries are distinct rows.
All inputs are finite; a program needn't handle non-finite values.
Results may differ from the reference program's by a relative error of at most 0.0085.
Values may be sent and summed in bfloat16 or wider, within the bound.
No kernel may reach another device: no remote copies, remote signals or barrier semaphores. Data moves between devices by JAX's collectives and lax.ppermute only.
A program may use at most 128 MiB of HBM per device.

```python
import jax
import jax.numpy as jnp
from jax import lax

D = 512
G_DEV = 2048
M_DEV = 80
MM_DEV = 640
CAP = 4
LAYERS = 2
G2M_FAN = 2
DEC_FAN = 3
GRID = 262144
MESH = 10240
MM_TOTAL = 81920
N_LAT = 8
N_LON = 16
DEVICES = 128


def neighbour_slots(key, fan):
    tile = jnp.arange(GRID, dtype=jnp.int32) // G_DEV
    tile_lat = tile // N_LON
    tile_lon = tile % N_LON
    first, second, third = jax.random.split(key, 3)
    step_lat = jax.random.randint(first, (fan, GRID), -1, 2)
    step_lon = jax.random.randint(second, (fan, GRID), -1, 2)
    outside_lat = (tile_lat + step_lat < 0) | (tile_lat + step_lat >= N_LAT)
    outside_lon = (tile_lon + step_lon < 0) | (tile_lon + step_lon >= N_LON)
    step_lat = jnp.where(outside_lat, 0, step_lat)
    step_lon = jnp.where(outside_lon, 0, step_lon)
    local_row = jax.random.randint(third, (fan, GRID), 0, M_DEV)
    return (((step_lat + 1) * 3 + step_lon + 1) * M_DEV + local_row).astype(jnp.int32)


def draw_encoder_slots(key, part):
    return neighbour_slots(jax.random.fold_in(key, 11), G2M_FAN)


def draw_decoder_slots(key, part):
    return neighbour_slots(jax.random.fold_in(key, 23), DEC_FAN)


def draw_peer_rows(key, part):
    keys = jax.random.split(jax.random.fold_in(key, 37), DEVICES * DEVICES)
    chosen = jax.vmap(lambda single: jax.random.permutation(single, M_DEV)[:CAP])(keys)
    return chosen.reshape(DEVICES, DEVICES, CAP).astype(jnp.int32)


def with_ends(array, own_key, low, largest):
    longest = array.shape.index(max(array.shape))
    spots = []
    for shift in (0, 1):
        where = [jax.random.randint(jax.random.fold_in(own_key, axis), (), 0, length) for axis, length in enumerate(array.shape)]
        where[longest] = (where[longest] + shift) % array.shape[longest]
        spots.append(tuple(where))
    return array.at[spots[0]].set(low).at[spots[1]].set(largest)


def level_of(stream_key, extent, cuts, smallest, high):
    level, own = 1.0, jax.random.fold_in(stream_key, 6)
    for position, parts in cuts:
        steps = jnp.exp(jax.random.uniform(jax.random.fold_in(own, position), (parts,), jnp.float32, smallest / len(cuts), high / len(cuts)))
        level = level * jnp.repeat(steps, extent[position] // parts).reshape([-1 if axis == position else 1 for axis in range(len(extent))])
    return level


def normal_values(key, extent, deviation, bound, cuts=(), kind=jnp.bfloat16):
    values = deviation * jax.random.normal(key, extent, jnp.float32)
    if cuts:
        values = values * level_of(key, extent, cuts, -0.22, 0.18)
    return jnp.clip(values, -bound, bound).astype(kind)


def setup_inputs(seed: int = 0) -> dict:
    streams_of = jax.random.split(jax.random.key(seed), 21)
    grid_latent = normal_values(streams_of[0], (GRID, D), 1.0, 6.0, ((0, 128),))
    mesh_latent = normal_values(streams_of[1], (MESH, D), 1.0, 6.0, ((0, 128),))
    encoder_slots = draw_encoder_slots(jax.random.fold_in(streams_of[20], 71), 0)
    decoder_slots = draw_decoder_slots(jax.random.fold_in(streams_of[20], 71), 0)
    peer_rows = draw_peer_rows(jax.random.fold_in(streams_of[20], 71), 0)
    edge_source = with_ends(jax.random.randint(streams_of[5], (MM_TOTAL,), 0, DEVICES * CAP), jax.random.fold_in(streams_of[5], 1), 0, (DEVICES * CAP) - 1).astype(jnp.int32)
    edge_target = with_ends(jax.random.randint(streams_of[6], (MM_TOTAL,), 0, M_DEV), jax.random.fold_in(streams_of[6], 1), 0, M_DEV - 1).astype(jnp.int32)
    encoder_sender = normal_values(streams_of[7], (D, D), D ** -0.5, 0.25)
    encoder_receiver = normal_values(streams_of[8], (D, D), D ** -0.5, 0.25)
    encoder_output = normal_values(streams_of[9], (D, D), D ** -0.5, 0.25)
    encoder_merge = normal_values(streams_of[10], (D, D), D ** -0.5, 0.25)
    encoder_self = normal_values(streams_of[11], (D, D), D ** -0.5, 0.25)
    process_sender = normal_values(streams_of[12], (LAYERS, D, D), D ** -0.5, 0.25)
    process_receiver = normal_values(streams_of[13], (LAYERS, D, D), D ** -0.5, 0.25)
    process_output = normal_values(streams_of[14], (LAYERS, D, D), D ** -0.5, 0.25)
    process_merge = normal_values(streams_of[15], (LAYERS, D, D), D ** -0.5, 0.25)
    process_self = normal_values(streams_of[16], (LAYERS, D, D), D ** -0.5, 0.25)
    decoder_sender = normal_values(streams_of[17], (D, D), D ** -0.5, 0.25)
    decoder_receiver = normal_values(streams_of[18], (D, D), D ** -0.5, 0.25)
    decoder_output = normal_values(streams_of[19], (D, D), D ** -0.5, 0.25)
    return dict(grid_latent=grid_latent, mesh_latent=mesh_latent, encoder_slots=encoder_slots, decoder_slots=decoder_slots, peer_rows=peer_rows, edge_source=edge_source, edge_target=edge_target, encoder_sender=encoder_sender, encoder_receiver=encoder_receiver, encoder_output=encoder_output, encoder_merge=encoder_merge, encoder_self=encoder_self, process_sender=process_sender, process_receiver=process_receiver, process_output=process_output, process_merge=process_merge, process_self=process_self, decoder_sender=decoder_sender, decoder_receiver=decoder_receiver, decoder_output=decoder_output)


def layer_norm(values):
    centre = values - lax.optimization_barrier(jnp.mean(values, axis=-1, keepdims=True))
    spread = lax.optimization_barrier(jnp.mean(centre * centre, axis=-1, keepdims=True))
    return centre * lax.rsqrt(spread + 1e-05)

def product(left, right):
    return jnp.dot(left, right, preferred_element_type=jnp.float32)

def mesh_index(slots, device):
    block = slots // M_DEV
    node_lat = device // N_LON + block // 3 - 1
    node_lon = device % N_LON + block % 3 - 1
    return ((node_lat * N_LON + node_lon) * M_DEV + slots % M_DEV).astype(jnp.int32)

def reference(grid_latent, mesh_latent, encoder_slots, decoder_slots, peer_rows, edge_source, edge_target, encoder_sender, encoder_receiver, encoder_output, encoder_merge, encoder_self, process_sender, process_receiver, process_output, process_merge, process_self, decoder_sender, decoder_receiver, decoder_output):
    width = grid_latent.shape[1]
    mesh_total = M_DEV * DEVICES
    tiles = jnp.arange(DEVICES, dtype=jnp.int32)
    grid_blocks = grid_latent.reshape(DEVICES, G_DEV, width)
    encoder_blocks = encoder_slots.reshape(G2M_FAN, DEVICES, G_DEV).transpose(1, 0, 2)
    decoder_blocks = decoder_slots.reshape(DEC_FAN, DEVICES, G_DEV).transpose(1, 0, 2)
    mesh_projected = product(mesh_latent, encoder_receiver)

    def encode(running, element):
        tile_rows, slots, device = element
        sender = product(tile_rows, encoder_sender)
        targets = mesh_index(slots, device)
        hidden = jax.nn.silu(sender[None] + mesh_projected[targets]).astype(jnp.bfloat16)
        message = product(hidden.reshape(-1, width), encoder_output)
        partial_value = jax.ops.segment_sum(message, targets.reshape(-1), num_segments=mesh_total)
        rounded = lax.optimization_barrier(partial_value.astype(jnp.bfloat16))
        return (running + rounded.astype(jnp.float32), None)
    start = jnp.zeros((mesh_total, width), jnp.float32)
    encoder_sum, _ = lax.scan(encode, start, (grid_blocks, encoder_blocks, tiles))
    update = product(encoder_sum.astype(jnp.bfloat16), encoder_merge) + product(mesh_latent, encoder_self)
    mesh_state = (mesh_latent.astype(jnp.float32) + layer_norm(jax.nn.silu(update))).astype(jnp.bfloat16)
    edge_tile = (jnp.arange(MM_DEV * DEVICES, dtype=jnp.int32) // MM_DEV).astype(jnp.int32)
    owner = (edge_source // CAP).astype(jnp.int32)
    source = (owner * M_DEV + peer_rows[edge_tile, owner, edge_source % CAP]).astype(jnp.int32)
    target = (edge_tile * M_DEV + edge_target).astype(jnp.int32)
    for depth in range(LAYERS):
        sent = lax.optimization_barrier(product(mesh_state, process_sender[depth]).astype(jnp.bfloat16))
        received = product(mesh_state, process_receiver[depth])
        hidden = jax.nn.silu(sent[source].astype(jnp.float32) + received[target]).astype(jnp.bfloat16)
        message = product(hidden, process_output[depth])
        process_sum = jax.ops.segment_sum(message, target, num_segments=mesh_total)
        update = product(process_sum.astype(jnp.bfloat16), process_merge[depth]) + product(mesh_state, process_self[depth])
        mesh_state = (mesh_state.astype(jnp.float32) + layer_norm(jax.nn.silu(update))).astype(jnp.bfloat16)
    decoded_mesh = product(mesh_state, decoder_sender)

    def decode(element):
        tile_rows, slots, device = element
        receiver = product(tile_rows, decoder_receiver)
        hidden = jax.nn.silu(decoded_mesh[mesh_index(slots, device)] + receiver[None]).astype(jnp.bfloat16)
        message = product(hidden.reshape(-1, width), decoder_output).reshape(DEC_FAN, -1, width)
        decoder_sum = lax.optimization_barrier(jnp.sum(message, axis=0))
        return (tile_rows.astype(jnp.float32) + layer_norm(decoder_sum)).astype(jnp.bfloat16)
    result = lax.map(decode, (grid_blocks, decoder_blocks, tiles))
    return result.reshape(DEVICES * G_DEV, width)
```

```python
import functools

import jax
import jax.numpy as jnp
from jax import lax
from jax.experimental import pallas as pl
from jax.experimental.pallas import tpu as pltpu
from jax.sharding import PartitionSpec as P

CAP = 4
LAYERS = 2
ENC_FAN = 2
DEC_FAN = 3
SIDE = 3
ENC_ROWS = 512
DEC_ROWS = 512
PRE_ROWS = 512


def up128(n):
    return -(-n // 128) * 128


def dot(left, right):
    return jnp.dot(left, right, preferred_element_type=jnp.float32)


def silu(v):
    half = 0.5 * v
    return half + half * jnp.tanh(half)


def norm(v):
    centre = v - jnp.mean(v, axis=-1, keepdims=True)
    spread = jnp.mean(centre * centre, axis=-1, keepdims=True)
    return centre * lax.rsqrt(spread + 1e-05)


def hot_rows(column, width):
    lanes = lax.broadcasted_iota(jnp.int32, (column.shape[0], width), 1)
    return jnp.where(lanes == column, 1.0, 0.0).astype(jnp.bfloat16)


def hot_columns(row, height):
    subs = lax.broadcasted_iota(jnp.int32, (height, row.shape[1]), 0)
    return jnp.where(subs == row, 1.0, 0.0).astype(jnp.bfloat16)


def bf(v):
    return v.astype(jnp.bfloat16)


def pre_kernel(grid_ref, ws_ref, dr_ref, s_ref, r_ref):
    g = grid_ref[...]
    s_ref[...] = bf(dot(g, ws_ref[...]))
    r_ref[...] = bf(dot(g, dr_ref[...]))


def pre(grid_latent, ws, dr):
    n, d = grid_latent.shape
    tile = pl.BlockSpec((PRE_ROWS, d), lambda i: (i, 0))
    whole = pl.BlockSpec((d, d), lambda i: (0, 0))
    return pl.pallas_call(
        pre_kernel,
        grid=(n // PRE_ROWS,),
        in_specs=[tile, whole, whole],
        out_specs=[tile, tile],
        out_shape=[jax.ShapeDtypeStruct((n, d), jnp.bfloat16)] * 2,
        name="pre",
    )(grid_latent, ws, dr)


def enc_kernel(s_ref, row_ref, col_ref, n0, n1, n2, wr_ref, out_ref, near, acc, hid):
    step = pl.program_id(0)
    rows = s_ref.shape[0]
    third = n0.shape[0]
    height = near.shape[0]

    @pl.when(step == 0)
    def _():
        w = wr_ref[...]
        for k, ref in enumerate((n0, n1, n2)):
            near[k * third : (k + 1) * third] = bf(dot(ref[...], w))
        near[SIDE * third :] = jnp.zeros((height - SIDE * third, near.shape[1]), jnp.bfloat16)
        acc[...] = jnp.zeros_like(acc)

    s = s_ref[...].astype(jnp.float32)
    for f in range(ENC_FAN):
        v = dot(hot_rows(col_ref[:, f : f + 1], height), near[...]) + s
        hid[f * rows : (f + 1) * rows] = bf(silu(v))
    chosen = jnp.concatenate(
        [hot_columns(row_ref[f : f + 1, :], height) for f in range(ENC_FAN)], axis=1
    )
    acc[...] += dot(chosen, hid[...])

    @pl.when(step == pl.num_programs(0) - 1)
    def _():
        out_ref[...] = bf(acc[: out_ref.shape[0]])


def encode(s, slot_rows, slot_cols, near, wr):
    n, d = s.shape
    third = near[0].shape[0]
    height = up128(SIDE * third)
    whole = pl.BlockSpec((third, d), lambda i: (0, 0))
    return pl.pallas_call(
        enc_kernel,
        grid=(n // ENC_ROWS,),
        in_specs=[
            pl.BlockSpec((ENC_ROWS, d), lambda i: (i, 0)),
            pl.BlockSpec((ENC_FAN, ENC_ROWS), lambda i: (0, i)),
            pl.BlockSpec((ENC_ROWS, ENC_FAN), lambda i: (i, 0)),
            whole,
            whole,
            whole,
            pl.BlockSpec((d, d), lambda i: (0, 0)),
        ],
        out_specs=pl.BlockSpec((SIDE * third, d), lambda i: (0, 0)),
        out_shape=jax.ShapeDtypeStruct((SIDE * third, d), jnp.bfloat16),
        scratch_shapes=[
            pltpu.VMEM((height, d), jnp.bfloat16),
            pltpu.VMEM((height, d), jnp.float32),
            pltpu.VMEM((ENC_FAN * ENC_ROWS, d), jnp.bfloat16),
        ],
        name="encode",
    )(s, slot_rows, slot_cols, *near, wr)


def merge_kernel(
    own_ref, a_ref, b_ref, mesh_ref, asked_ref, wo, wm, wself, ws, state_ref, out_ref
):
    mesh = mesh_ref[...]
    total = own_ref[...] + a_ref[...].astype(jnp.float32) + b_ref[...].astype(jnp.float32)
    summed = bf(dot(bf(total), wo[...]))
    update = dot(summed, wm[...]) + dot(mesh, wself[...])
    state = bf(mesh.astype(jnp.float32) + norm(silu(update)))
    state_ref[...] = state
    sent = bf(dot(state, ws[...]))
    out_ref[...] = bf(dot(hot_rows(asked_ref[...], state.shape[0]), sent))


def merge(own, a, b, mesh, asked, wo, wm, wself, ws):
    rows, d = mesh.shape
    return pl.pallas_call(
        merge_kernel,
        out_shape=[
            jax.ShapeDtypeStruct((rows, d), jnp.bfloat16),
            jax.ShapeDtypeStruct((asked.shape[0], d), jnp.bfloat16),
        ],
        name="merge",
    )(own, a, b, mesh, asked, wo, wm, wself, ws)


def layer_kernel(
    last, in_ref, state_ref, src_ref, tgt_ref, tgt_row_ref, asked_ref, wr, wo, wm, wself, wn, *outs
):
    state = state_ref[...]
    owned = state.shape[0]
    received = bf(dot(state, wr[...]))
    v = dot(hot_rows(src_ref[...], in_ref.shape[0]), in_ref[...])
    v += dot(hot_rows(tgt_ref[...], owned), received)
    hidden = bf(silu(v))
    gathered = dot(hot_columns(tgt_row_ref[...], owned), hidden)
    summed = bf(dot(bf(gathered), wo[...]))
    update = dot(summed, wm[...]) + dot(state, wself[...])
    new = bf(state.astype(jnp.float32) + norm(silu(update)))
    sent = bf(dot(new, wn[...]))
    if last:
        outs[0][...] = sent
    else:
        outs[0][...] = new
        outs[1][...] = bf(dot(hot_rows(asked_ref[...], owned), sent))


def layer(last, incoming, state, src, tgt, tgt_row, asked, wr, wo, wm, wself, wn):
    rows, d = state.shape
    out = [jax.ShapeDtypeStruct((rows, d), jnp.bfloat16)]
    if not last:
        out.append(jax.ShapeDtypeStruct((asked.shape[0], d), jnp.bfloat16))
    return pl.pallas_call(
        functools.partial(layer_kernel, last),
        out_shape=out,
        name="layer_last" if last else "layer_first",
    )(incoming, state, src, tgt, tgt_row, asked, wr, wo, wm, wself, wn)


def dec_kernel(r_ref, grid_ref, col_ref, n0, n1, n2, wo, out_ref, near):
    third = n0.shape[0]
    height = near.shape[0]

    @pl.when(pl.program_id(0) == 0)
    def _():
        for k, ref in enumerate((n0, n1, n2)):
            near[k * third : (k + 1) * third] = ref[...]
        near[SIDE * third :] = jnp.zeros((height - SIDE * third, near.shape[1]), jnp.bfloat16)

    r = r_ref[...].astype(jnp.float32)
    total = None
    for f in range(DEC_FAN):
        v = dot(hot_rows(col_ref[:, f : f + 1], height), near[...]) + r
        h = bf(silu(v)).astype(jnp.float32)
        total = h if total is None else total + h
    high = bf(total)
    low = bf(total - high.astype(jnp.float32))
    w = wo[...]
    update = dot(high, w) + dot(low, w)
    out_ref[...] = bf(grid_ref[...].astype(jnp.float32) + norm(update))


def decode(r, grid_latent, slot_cols, near, wo):
    n, d = r.shape
    third = near[0].shape[0]
    height = up128(SIDE * third)
    whole = pl.BlockSpec((third, d), lambda i: (0, 0))
    tile = pl.BlockSpec((DEC_ROWS, d), lambda i: (i, 0))
    return pl.pallas_call(
        dec_kernel,
        grid=(n // DEC_ROWS,),
        in_specs=[
            tile,
            tile,
            pl.BlockSpec((DEC_ROWS, DEC_FAN), lambda i: (i, 0)),
            whole,
            whole,
            whole,
            pl.BlockSpec((d, d), lambda i: (0, 0)),
        ],
        out_specs=tile,
        out_shape=jax.ShapeDtypeStruct((n, d), jnp.bfloat16),
        scratch_shapes=[pltpu.VMEM((height, d), jnp.bfloat16)],
        name="decode",
    )(r, grid_latent, slot_cols, *near, wo)


def swaps(axis):
    count = lax.axis_size(axis)
    first = [(i, i ^ 1) for i in range(count)]
    second = []
    for i in range(1, count - 1, 2):
        second += [(i, i + 1), (i + 1, i)]
    return first, second


def swap_both(axis, to_first, to_second):
    first, second = swaps(axis)
    b = lax.ppermute(to_second, axis, second)
    a = lax.ppermute(to_first, axis, first)
    return a, b


def neighbours(rows):
    a, b = swap_both("lon", rows, rows)
    line = jnp.concatenate([rows, a, b], axis=0)
    c, d = swap_both("lat", line, line)
    return line, c, d


def to_owners(partial_sums):
    a, b = swap_both("lat", partial_sums[1], partial_sums[2])
    line = (
        partial_sums[0].astype(jnp.float32) + a.astype(jnp.float32) + b.astype(jnp.float32)
    )
    c, d = swap_both("lon", bf(line[1]), bf(line[2]))
    return line[0], c, d


def place(offset, axis):
    odd = lax.axis_index(axis) % 2
    return jnp.where(odd == 1, (4 - offset) % 3, (offset + 2) % 3)


def exchange_slots(slots, owned):
    block, row = slots // owned, slots % owned
    return (place(block // 3, "lat") * 3 + place(block % 3, "lon")) * owned + row


def local(
    grid_latent,
    mesh_latent,
    encoder_slots,
    decoder_slots,
    peer_rows,
    edge_source,
    edge_target,
    encoder_sender,
    encoder_receiver,
    encoder_output,
    encoder_merge,
    encoder_self,
    process_sender,
    process_receiver,
    process_output,
    process_merge,
    process_self,
    decoder_sender,
    decoder_receiver,
    decoder_output,
):
    owned, width = mesh_latent.shape
    wanted = peer_rows[0]
    tiles = wanted.shape[0]
    near = neighbours(mesh_latent)
    asked = lax.all_to_all(wanted, ("lat", "lon"), split_axis=0, concat_axis=0, tiled=True)
    asked = asked.reshape(tiles * CAP, 1)
    s, r = pre(grid_latent, encoder_sender, decoder_receiver)
    enc = exchange_slots(encoder_slots, owned)
    dec = exchange_slots(decoder_slots, owned)
    partial_sums = encode(s, enc, enc.T, near, encoder_receiver)
    own, a, b = to_owners(partial_sums.reshape(SIDE, SIDE, owned, width))
    state, outgoing = merge(
        own,
        a,
        b,
        mesh_latent,
        asked,
        encoder_output,
        encoder_merge,
        encoder_self,
        process_sender[0],
    )
    src = edge_source[:, None]
    tgt = edge_target[:, None]
    tgt_row = edge_target[None, :]
    for depth in range(LAYERS):
        last = depth == LAYERS - 1
        incoming = lax.all_to_all(
            outgoing.reshape(tiles, CAP, width),
            ("lat", "lon"),
            split_axis=0,
            concat_axis=0,
            tiled=True,
        ).reshape(tiles * CAP, width)
        result = layer(
            last,
            incoming,
            state,
            src,
            tgt,
            tgt_row,
            asked,
            process_receiver[depth],
            process_output[depth],
            process_merge[depth],
            process_self[depth],
            decoder_sender if last else process_sender[depth + 1],
        )
        if not last:
            state, outgoing = result
    return decode(r, grid_latent, dec.T, neighbours(result[0]), decoder_output)


def solution(mesh):
    return jax.shard_map(
        local,
        mesh=mesh,
        in_specs=(
            P(("lat", "lon"), None),
            P(("lat", "lon"), None),
            P(None, ("lat", "lon")),
            P(None, ("lat", "lon")),
            P(("lat", "lon"), None, None),
            P(("lat", "lon")),
            P(("lat", "lon")),
            P(),
            P(),
            P(),
            P(),
            P(),
            P(),
            P(),
            P(),
            P(),
            P(),
            P(),
            P(),
            P(),
        ),
        out_specs=P(("lat", "lon"), None),
        check_vma=False,
    )
```

```python
import functools

import jax
import jax.numpy as jnp
from jax import lax
from jax.experimental import pallas as pl
from jax.experimental.pallas import tpu as pltpu
from jax.sharding import PartitionSpec as P

CAP = 4
LAYERS = 2
ENC_FAN = 2
DEC_FAN = 3
SIDE = 3
ENC_ROWS = 1024
DEC_ROWS = 512
PRE_ROWS = 1024


def up128(n):
    return -(-n // 128) * 128


def dot(left, right):
    return jnp.dot(left, right, preferred_element_type=jnp.float32)


def silu(v):
    half = 0.5 * v
    return half + half * jnp.tanh(half)


def norm(v):
    centre = v - jnp.mean(v, axis=-1, keepdims=True)
    spread = jnp.mean(centre * centre, axis=-1, keepdims=True)
    return centre * lax.rsqrt(spread + 1e-05)


def hot_rows(row, width):
    n = row.shape[1]
    columns = jnp.broadcast_to(row, (128, n)).T
    lanes = lax.broadcasted_iota(jnp.int32, (n, 128), 1)
    parts = [
        jnp.where(lanes + at == columns, 1.0, 0.0).astype(jnp.bfloat16)
        for at in range(0, width, 128)
    ]
    return jnp.concatenate(parts, axis=1) if len(parts) > 1 else parts[0]


def hot_columns(row, height):
    subs = lax.broadcasted_iota(jnp.int32, (height, row.shape[1]), 0)
    return jnp.where(subs == row, 1.0, 0.0).astype(jnp.bfloat16)


def bf(v):
    return v.astype(jnp.bfloat16)


def pre_kernel(grid_ref, ws_ref, dr_ref, s_ref, r_ref):
    g = grid_ref[...]
    s_ref[...] = bf(dot(g, ws_ref[...]))
    r_ref[...] = bf(dot(g, dr_ref[...]))


def pre(grid_latent, ws, dr):
    n, d = grid_latent.shape
    tile = pl.BlockSpec((PRE_ROWS, d), lambda i: (i, 0))
    whole = pl.BlockSpec((d, d), lambda i: (0, 0))
    return pl.pallas_call(
        pre_kernel,
        grid=(n // PRE_ROWS,),
        in_specs=[tile, whole, whole],
        out_specs=[tile, tile],
        out_shape=[jax.ShapeDtypeStruct((n, d), jnp.bfloat16)] * 2,
        name="pre",
    )(grid_latent, ws, dr)


def block_at(odd_ref, place):
    spots = []
    for axis, at in enumerate((place // SIDE, place % SIDE)):
        odd = odd_ref[axis]
        spots.append((1, 2 - 2 * odd, 2 * odd)[at])
    return spots[0] * SIDE + spots[1]


def enc_kernel(odd_ref, s_ref, slots_ref, n0, n1, n2, wr_ref, o0, o1, o2, near, acc, hid):
    step = pl.program_id(0)
    rows = s_ref.shape[0]
    owned = n0.shape[0] // SIDE
    height = near.shape[0]
    slots = SIDE * SIDE * owned

    def block(k, at):
        start = pl.multiple_of(block_at(odd_ref, k * SIDE + at) * owned, 16)
        return pl.ds(start, owned)

    @pl.when(step == 0)
    def _():
        w = wr_ref[...]
        for k, ref in enumerate((n0, n1, n2)):
            v = bf(dot(ref[...], w))
            for at in range(SIDE):
                near[block(k, at), :] = v[at * owned : (at + 1) * owned]
        near[slots:] = jnp.zeros((height - slots, near.shape[1]), jnp.bfloat16)
        acc[...] = jnp.zeros_like(acc)

    s = s_ref[...].astype(jnp.float32)
    for f in range(ENC_FAN):
        v = dot(hot_rows(slots_ref[f : f + 1, :], height), near[...]) + s
        hid[f * rows : (f + 1) * rows] = bf(silu(v))
    chosen = jnp.concatenate(
        [hot_columns(slots_ref[f : f + 1, :], slots) for f in range(ENC_FAN)], axis=1
    )
    acc[...] += dot(chosen, hid[...])

    @pl.when(step == pl.num_programs(0) - 1)
    def _():
        for k, ref in enumerate((o0, o1, o2)):
            for at in range(SIDE):
                ref[at * owned : (at + 1) * owned] = bf(acc[block(k, at), :])


def encode(odd, s, slot_rows, near, wr):
    n, d = s.shape
    third = near[0].shape[0]
    height = up128(SIDE * third)
    whole = pl.BlockSpec((third, d), lambda i: (0, 0))
    return pl.pallas_call(
        enc_kernel,
        grid=(n // ENC_ROWS,),
        in_specs=[
            pl.BlockSpec(memory_space=pltpu.SMEM),
            pl.BlockSpec((ENC_ROWS, d), lambda i: (i, 0)),
            pl.BlockSpec((ENC_FAN, ENC_ROWS), lambda i: (0, i)),
            whole,
            whole,
            whole,
            pl.BlockSpec((d, d), lambda i: (0, 0)),
        ],
        out_specs=[whole] * SIDE,
        out_shape=[jax.ShapeDtypeStruct((third, d), jnp.bfloat16)] * SIDE,
        scratch_shapes=[
            pltpu.VMEM((height, d), jnp.bfloat16),
            pltpu.VMEM((SIDE * third, d), jnp.float32),
            pltpu.VMEM((ENC_FAN * ENC_ROWS, d), jnp.bfloat16),
        ],
        name="encode",
    )(odd, s, slot_rows, *near, wr)


def pack(rows, wide, out_ref):
    n, d = rows.shape
    parts = d // 128
    for c in range(parts):
        wide[pl.ds(c, n, stride=parts), :] = rows[:, c * 128 : (c + 1) * 128]
    out_ref[...] = bf(wide[...])


def unpack(in_ref, wide, d):
    parts = d // 128
    n = in_ref.shape[0] // parts
    wide[...] = in_ref[...].astype(jnp.float32)
    return jnp.concatenate(
        [bf(wide[pl.ds(c, n, stride=parts), :]) for c in range(parts)], axis=1
    )


def padded_rows(rows):
    extra = up128(rows.shape[0]) - rows.shape[0]
    return jnp.concatenate([rows, jnp.zeros((extra, rows.shape[1]), rows.dtype)], axis=0)


def merge_kernel(
    o_ref, a_ref, b_ref, mesh_ref, asked_ref, wo, wm, wself, ws, state_ref, out_ref, wide
):
    mesh = mesh_ref[...]
    total = o_ref[...] + a_ref[...].astype(jnp.float32) + b_ref[...].astype(jnp.float32)
    summed = bf(dot(bf(total), wo[...]))
    update = dot(summed, wm[...]) + dot(mesh, wself[...])
    state = bf(mesh.astype(jnp.float32) + norm(silu(update)))
    state_ref[...] = state
    sent = padded_rows(bf(dot(state, ws[0])))
    pack(dot(hot_rows(asked_ref[...], sent.shape[0]), sent), wide, out_ref)


def whole_spec(shape):
    return pl.BlockSpec(shape, lambda i: (0,) * len(shape))


def depth_spec(shape, depth):
    return pl.BlockSpec((1,) + shape[1:], lambda i: (depth,) + (0,) * (len(shape) - 1))


def merge(own, a, b, mesh, asked, wo, wm, wself, ws):
    rows, d = mesh.shape
    entries = asked.shape[1]
    args = (own, a, b, mesh, asked, wo, wm, wself)
    packed = (entries * d // 128, 128)
    return pl.pallas_call(
        merge_kernel,
        grid=(1,),
        in_specs=[whole_spec(x.shape) for x in args] + [depth_spec(ws.shape, 0)],
        out_specs=[whole_spec((rows, d)), whole_spec(packed)],
        out_shape=[
            jax.ShapeDtypeStruct((rows, d), jnp.bfloat16),
            jax.ShapeDtypeStruct(packed, jnp.bfloat16),
        ],
        scratch_shapes=[pltpu.VMEM(packed, jnp.float32)],
        name="merge",
    )(*args, ws)


def ready_kernel(state_ref, tgt_ref, wr, wself, base_ref, self_ref):
    state = state_ref[...]
    received = padded_rows(bf(dot(state, wr[0])))
    base_ref[...] = bf(dot(hot_rows(tgt_ref[...], received.shape[0]), received))
    self_ref[...] = dot(state, wself[0])


def ready(depth, state, tgt, wr, wself):
    rows, d = state.shape
    edges = tgt.shape[1]
    return pl.pallas_call(
        ready_kernel,
        grid=(1,),
        in_specs=[
            whole_spec(state.shape),
            whole_spec(tgt.shape),
            depth_spec(wr.shape, depth),
            depth_spec(wself.shape, depth),
        ],
        out_specs=[whole_spec((edges, d)), whole_spec((rows, d))],
        out_shape=[
            jax.ShapeDtypeStruct((edges, d), jnp.bfloat16),
            jax.ShapeDtypeStruct((rows, d), jnp.float32),
        ],
        name="ready",
    )(state, tgt, wr, wself)


def layer_kernel(
    last, in_ref, base_ref, self_ref, state_ref, src_ref, tgt_ref, asked_ref, wo, wm, wn, *rest
):
    outs, wide = rest[:-1], rest[-1]
    owned, d = state_ref.shape
    incoming = unpack(in_ref, wide, d)
    v = dot(hot_rows(src_ref[...], incoming.shape[0]), incoming)
    hidden = bf(silu(v + base_ref[...].astype(jnp.float32)))
    gathered = dot(hot_columns(tgt_ref[...], owned), hidden)
    summed = bf(dot(bf(gathered), wo[0]))
    update = dot(summed, wm[0]) + self_ref[...]
    new = bf(state_ref[...].astype(jnp.float32) + norm(silu(update)))
    if last:
        outs[0][...] = bf(dot(new, wn[...]))
    else:
        outs[0][...] = new
        sent = padded_rows(bf(dot(new, wn[0])))
        pack(dot(hot_rows(asked_ref[...], sent.shape[0]), sent), wide, outs[1])


def layer(depth, last, incoming, base, own, state, src, tgt, asked, wo, wm, wn):
    rows, d = state.shape
    args = (incoming, base, own, state, src, tgt, asked)
    out = [jax.ShapeDtypeStruct((rows, d), jnp.bfloat16)]
    if not last:
        out.append(jax.ShapeDtypeStruct(incoming.shape, jnp.bfloat16))
    return pl.pallas_call(
        functools.partial(layer_kernel, last),
        grid=(1,),
        in_specs=[whole_spec(x.shape) for x in args]
        + [
            depth_spec(wo.shape, depth),
            depth_spec(wm.shape, depth),
            whole_spec(wn.shape) if last else depth_spec(wn.shape, depth + 1),
        ],
        out_specs=[whole_spec(x.shape) for x in out],
        out_shape=out,
        scratch_shapes=[pltpu.VMEM(incoming.shape, jnp.float32)],
        name="layer_last" if last else "layer_first",
    )(*args, wo, wm, wn)


def dec_kernel(odd_ref, r_ref, grid_ref, slots_ref, n0, n1, n2, wo, out_ref, near):
    owned = n0.shape[0] // SIDE
    height = near.shape[0]
    slots = SIDE * SIDE * owned

    @pl.when(pl.program_id(0) == 0)
    def _():
        for k, ref in enumerate((n0, n1, n2)):
            for at in range(SIDE):
                start = pl.multiple_of(block_at(odd_ref, k * SIDE + at) * owned, 16)
                near[pl.ds(start, owned), :] = ref[at * owned : (at + 1) * owned]
        near[slots:] = jnp.zeros((height - slots, near.shape[1]), jnp.bfloat16)

    r = r_ref[...].astype(jnp.float32)
    total = None
    for f in range(DEC_FAN):
        v = dot(hot_rows(slots_ref[f : f + 1, :], height), near[...]) + r
        h = bf(silu(v)).astype(jnp.float32)
        total = h if total is None else total + h
    update = dot(bf(total), wo[...])
    out_ref[...] = bf(grid_ref[...].astype(jnp.float32) + norm(update))


def decode(odd, r, grid_latent, slot_rows, near, wo):
    n, d = r.shape
    third = near[0].shape[0]
    height = up128(SIDE * third)
    whole = pl.BlockSpec((third, d), lambda i: (0, 0))
    tile = pl.BlockSpec((DEC_ROWS, d), lambda i: (i, 0))
    return pl.pallas_call(
        dec_kernel,
        grid=(n // DEC_ROWS,),
        in_specs=[
            pl.BlockSpec(memory_space=pltpu.SMEM),
            tile,
            tile,
            pl.BlockSpec((DEC_FAN, DEC_ROWS), lambda i: (0, i)),
            whole,
            whole,
            whole,
            pl.BlockSpec((d, d), lambda i: (0, 0)),
        ],
        out_specs=tile,
        out_shape=jax.ShapeDtypeStruct((n, d), jnp.bfloat16),
        scratch_shapes=[pltpu.VMEM((height, d), jnp.bfloat16)],
        name="decode",
    )(odd, r, grid_latent, slot_rows, *near, wo)


def swaps(axis):
    count = lax.axis_size(axis)
    first = [(i, i ^ 1) for i in range(count)]
    second = []
    for i in range(1, count - 1, 2):
        second += [(i, i + 1), (i + 1, i)]
    return first, second


def swap_both(axis, to_first, to_second):
    first, second = swaps(axis)
    b = lax.ppermute(to_second, axis, second)
    a = lax.ppermute(to_first, axis, first)
    return a, b


def neighbours(rows):
    a, b = swap_both("lon", rows, rows)
    line = jnp.concatenate([rows, a, b], axis=0)
    c, d = swap_both("lat", line, line)
    return line, c, d


def to_owners(sums, owned):
    a, b = swap_both("lat", sums[1], sums[2])

    def line(at):
        part = slice(at * owned, (at + 1) * owned)
        return (
            sums[0][part].astype(jnp.float32)
            + a[part].astype(jnp.float32)
            + b[part].astype(jnp.float32)
        )

    c, d = swap_both("lon", bf(line(1)), bf(line(2)))
    return line(0), c, d


def local(
    grid_latent,
    mesh_latent,
    encoder_slots,
    decoder_slots,
    peer_rows,
    edge_source,
    edge_target,
    encoder_sender,
    encoder_receiver,
    encoder_output,
    encoder_merge,
    encoder_self,
    process_sender,
    process_receiver,
    process_output,
    process_merge,
    process_self,
    decoder_sender,
    decoder_receiver,
    decoder_output,
):
    owned, width = mesh_latent.shape
    wanted = peer_rows[0]
    tiles = wanted.shape[0]
    odd = jnp.stack([lax.axis_index("lat") % 2, lax.axis_index("lon") % 2]).astype(jnp.int32)
    near = neighbours(mesh_latent)
    asked = lax.all_to_all(wanted, ("lat", "lon"), split_axis=0, concat_axis=0, tiled=True)
    asked = asked.reshape(1, tiles * CAP)
    s, r = pre(grid_latent, encoder_sender, decoder_receiver)
    sums = encode(odd, s, encoder_slots, near, encoder_receiver)
    own, a, b = to_owners(sums, owned)
    state, outgoing = merge(
        own,
        a,
        b,
        mesh_latent,
        asked,
        encoder_output,
        encoder_merge,
        encoder_self,
        process_sender,
    )
    src = edge_source[None, :]
    tgt = edge_target[None, :]
    for depth in range(LAYERS):
        last = depth == LAYERS - 1
        incoming = lax.all_to_all(
            outgoing.reshape(tiles, -1, 128),
            ("lat", "lon"),
            split_axis=0,
            concat_axis=0,
            tiled=True,
        ).reshape(outgoing.shape)
        base, self_part = ready(depth, state, tgt, process_receiver, process_self)
        result = layer(
            depth,
            last,
            incoming,
            base,
            self_part,
            state,
            src,
            tgt,
            asked,
            process_output,
            process_merge,
            decoder_sender if last else process_sender,
        )
        if not last:
            state, outgoing = result
    return decode(odd, r, grid_latent, decoder_slots, neighbours(result[0]), decoder_output)


def solution(mesh):
    return jax.shard_map(
        local,
        mesh=mesh,
        in_specs=(
            P(("lat", "lon"), None),
            P(("lat", "lon"), None),
            P(None, ("lat", "lon")),
            P(None, ("lat", "lon")),
            P(("lat", "lon"), None, None),
            P(("lat", "lon")),
            P(("lat", "lon")),
            P(),
            P(),
            P(),
            P(),
            P(),
            P(),
            P(),
            P(),
            P(),
            P(),
            P(),
            P(),
            P(),
        ),
        out_specs=P(("lat", "lon"), None),
        check_vma=False,
    )
```

```python
import functools

import jax
import jax.numpy as jnp
from jax import lax
from jax.experimental import pallas as pl
from jax.experimental.pallas import tpu as pltpu
from jax.sharding import PartitionSpec as P


LAYERS = 2
ENC_FAN = 2
DEC_FAN = 3
SIDE = 3
ENC_ROWS = 1024
DEC_ROWS = 512
PRE_ROWS = 512


def up128(n):
    return -(-n // 128) * 128


def dot(left, right):
    return jnp.dot(left, right, preferred_element_type=jnp.float32)


def silu(v):
    half = 0.5 * v
    return half + half * jnp.tanh(half)


def norm(v):
    centre = v - jnp.mean(v, axis=-1, keepdims=True)
    spread = jnp.mean(centre * centre, axis=-1, keepdims=True)
    return centre * lax.rsqrt(spread + 1e-05)


def hot_rows(row, width):
    n = row.shape[1]
    columns = jnp.broadcast_to(row, (128, n)).T
    lanes = lax.broadcasted_iota(jnp.int32, (n, 128), 1)
    parts = [
        jnp.where(lanes + at == columns, 1.0, 0.0).astype(jnp.bfloat16)
        for at in range(0, width, 128)
    ]
    return jnp.concatenate(parts, axis=1) if len(parts) > 1 else parts[0]


def hot_columns(row, height):
    subs = lax.broadcasted_iota(jnp.int32, (height, row.shape[1]), 0)
    return jnp.where(subs == row, 1.0, 0.0).astype(jnp.bfloat16)


def bf(v):
    return v.astype(jnp.bfloat16)


VMEM = pl.BlockSpec(memory_space=pltpu.VMEM)
HBM = pl.BlockSpec(memory_space=pltpu.HBM)


def near_to(space, arrays):
    return [pltpu.with_memory_space_constraint(x, space) for x in arrays]


def on_chip(kernel, args, outs, far=(), scratch=(), odd=None, limit=16):
    args = near_to(pltpu.VMEM, args)
    specs = [VMEM] * len(args) + [HBM] * len(far)
    args += near_to(pltpu.HBM, far)
    if odd is not None:
        args = [odd] + args
        specs = [pl.BlockSpec(memory_space=pltpu.SMEM)] + specs
    return pl.pallas_call(
        kernel,
        in_specs=specs,
        out_specs=[VMEM] * len(outs),
        out_shape=[pltpu.VMEM(shape, dtype) for shape, dtype in outs],
        scratch_shapes=list(scratch),
        compiler_params=pltpu.CompilerParams(vmem_limit_bytes=limit << 20),
    )(*args)


def fetch(pairs, sems):
    copies = [pltpu.make_async_copy(x, y, sems.at[i]) for i, (x, y) in enumerate(pairs)]
    for copy in copies:
        copy.start()
    return copies


def pre_kernel(
    grid_ref, ws_ref, dr_ref, wr_ref, slots_ref, s_ref, wr_out, slots_out, r_ref, w, g, r, sems
):
    rows = PRE_ROWS
    count = grid_ref.shape[0] // rows
    parts = [slice(i * rows, (i + 1) * rows) for i in range(count)]
    pairs = [(ws_ref, w.at[0]), (dr_ref, w.at[1])]
    pairs += [(grid_ref.at[part], g.at[part]) for part in parts]
    pairs += [(wr_ref, wr_out), (slots_ref, slots_out)]
    copies = fetch(pairs, sems)
    copies[0].wait()
    copies[1].wait()
    backs = []
    for i, part in enumerate(parts):
        copies[2 + i].wait()
        x = g[part]
        s_ref[part] = bf(dot(x, w[0]))
        r[part] = bf(dot(x, w[1]))
        backs.append(
            pltpu.make_async_copy(r.at[part], r_ref.at[part], sems.at[len(pairs) + i])
        )
        backs[-1].start()
    for copy in copies[2 + count :] + backs:
        copy.wait()


def pre(grid_latent, ws, dr, wr, slots):
    n, d = grid_latent.shape
    args = near_to(pltpu.HBM, [grid_latent, ws, dr, wr, slots])
    return pl.pallas_call(
        pre_kernel,
        in_specs=[HBM] * len(args),
        out_specs=[VMEM] * 3 + [HBM],
        out_shape=[
            pltpu.VMEM((n, d), jnp.bfloat16),
            pltpu.VMEM((d, d), jnp.bfloat16),
            pltpu.VMEM(slots.shape, jnp.int32),
            pltpu.HBM((n, d), jnp.bfloat16),
        ],
        scratch_shapes=[
            pltpu.VMEM((2, d, d), jnp.bfloat16),
            pltpu.VMEM((n, d), jnp.bfloat16),
            pltpu.VMEM((n, d), jnp.bfloat16),
            pltpu.SemaphoreType.DMA((4 + 2 * (n // PRE_ROWS),)),
        ],
        compiler_params=pltpu.CompilerParams(vmem_limit_bytes=20 << 20),
        name="pre",
    )(*args)


def block_at(odd_ref, place):
    spots = []
    for axis, at in enumerate((place // SIDE, place % SIDE)):
        odd = odd_ref[axis]
        spots.append((1, 2 - 2 * odd, 2 * odd)[at])
    return spots[0] * SIDE + spots[1]


def enc_kernel(odd_ref, s_ref, slots_ref, n0, n1, n2, wr_ref, o0, o1, o2, near, acc, hid):
    rows = hid.shape[0] // ENC_FAN
    owned = n0.shape[0] // SIDE
    height = near.shape[0]
    slots = SIDE * SIDE * owned

    def block(k, at):
        start = pl.multiple_of(block_at(odd_ref, k * SIDE + at) * owned, 16)
        return pl.ds(start, owned)

    w = wr_ref[...]
    for k, ref in enumerate((n0, n1, n2)):
        v = bf(dot(ref[...], w))
        for at in range(SIDE):
            near[block(k, at), :] = v[at * owned : (at + 1) * owned]
    near[slots:] = jnp.zeros((height - slots, near.shape[1]), jnp.bfloat16)

    for step in range(s_ref.shape[0] // rows):
        part = slice(step * rows, (step + 1) * rows)
        s = s_ref[part].astype(jnp.float32)
        for f in range(ENC_FAN):
            v = dot(hot_rows(slots_ref[f : f + 1, part], height), near[...]) + s
            hid[f * rows : (f + 1) * rows] = bf(silu(v))
        chosen = jnp.concatenate(
            [hot_columns(slots_ref[f : f + 1, part], slots) for f in range(ENC_FAN)], axis=1
        )
        sums = dot(chosen, hid[...])
        acc[...] = sums if step == 0 else acc[...] + sums

    for k, ref in enumerate((o0, o1, o2)):
        for at in range(SIDE):
            ref[at * owned : (at + 1) * owned] = bf(acc[block(k, at), :])


def encode(odd, s, slot_rows, near, wr):
    _, d = s.shape
    third = near[0].shape[0]
    height = up128(SIDE * third)
    return on_chip(
        enc_kernel,
        [s, slot_rows, *near, wr],
        [((third, d), jnp.bfloat16)] * SIDE,
        scratch=[
            pltpu.VMEM((height, d), jnp.bfloat16),
            pltpu.VMEM((SIDE * third, d), jnp.float32),
            pltpu.VMEM((ENC_FAN * ENC_ROWS, d), jnp.bfloat16),
        ],
        odd=odd,
        limit=28,
    )


def pack(sent, asked_ref, wide, out_ref):
    sent = padded_rows(bf(sent))
    tiles, cap = asked_ref.shape
    parts = sent.shape[1] // 128
    lanes = lax.broadcasted_iota(jnp.int32, (tiles, sent.shape[0]), 1)
    for k in range(cap):
        chosen = bf(jnp.where(lanes == asked_ref[:, k : k + 1], 1.0, 0.0))
        rows = dot(chosen, sent)
        for c in range(parts):
            wide[pl.ds(k * parts + c, tiles, stride=cap * parts), :] = rows[
                :, c * 128 : (c + 1) * 128
            ]
    out_ref[...] = bf(wide[...])


def unpack(in_ref, wide, d):
    parts = d // 128
    n = in_ref.shape[0] // parts
    wide[...] = in_ref[...].astype(jnp.float32)
    return jnp.concatenate(
        [bf(wide[pl.ds(c, n, stride=parts), :]) for c in range(parts)], axis=1
    )


def padded_rows(rows):
    extra = up128(rows.shape[0]) - rows.shape[0]
    return jnp.concatenate([rows, jnp.zeros((extra, rows.shape[1]), rows.dtype)], axis=0)


def stage_kernel(mesh, wo, wm, wself, ws, wo_out, wm_out, ws_out, self_ref, w, sems):
    copies = fetch([(wself, w), (wo, wo_out), (wm, wm_out), (ws.at[0], ws_out)], sems)
    copies[0].wait()
    self_ref[...] = dot(mesh[...], w[...])
    for copy in copies[1:]:
        copy.wait()


def stage(mesh, wo, wm, wself, ws):
    rows, d = mesh.shape
    return on_chip(
        stage_kernel,
        [mesh],
        [((d, d), jnp.bfloat16)] * 3 + [((rows, d), jnp.float32)],
        far=[wo, wm, wself, ws],
        scratch=[pltpu.VMEM((d, d), jnp.bfloat16), pltpu.SemaphoreType.DMA((4,))],
    )


def merge_kernel(
    o_ref, a_ref, b_ref, mesh_ref, asked_ref, wo, wm, ws, self_ref, state_ref, out_ref, wide
):
    total = o_ref[...] + a_ref[...].astype(jnp.float32) + b_ref[...].astype(jnp.float32)
    summed = bf(dot(bf(total), wo[...]))
    update = dot(summed, wm[...]) + self_ref[...]
    state = bf(mesh_ref[...].astype(jnp.float32) + norm(silu(update)))
    state_ref[...] = state
    pack(dot(state, ws[...]), asked_ref, wide, out_ref)


def merge(own, a, b, mesh, asked, staged):
    packed = (asked.size * mesh.shape[1] // 128, 128)
    return on_chip(
        merge_kernel,
        [own, a, b, mesh, asked, *staged],
        [(mesh.shape, jnp.bfloat16), (packed, jnp.bfloat16)],
        scratch=[pltpu.VMEM(packed, jnp.float32)],
    )


def ready_kernel(depth, state_ref, tgt_ref, wr, wself, base_ref, self_ref, w, sems):
    copies = fetch([(wr.at[depth], w.at[0]), (wself.at[depth], w.at[1])], sems)
    state = state_ref[...]
    chosen = hot_rows(tgt_ref[...], up128(state.shape[0]))
    copies[0].wait()
    received = padded_rows(bf(dot(state, w[0])))
    base_ref[...] = bf(dot(chosen, received))
    copies[1].wait()
    self_ref[...] = dot(state, w[1])


def ready(depth, state, tgt, wr, wself):
    rows, d = state.shape
    return on_chip(
        functools.partial(ready_kernel, depth),
        [state, tgt],
        [((tgt.shape[1], d), jnp.bfloat16), ((rows, d), jnp.float32)],
        far=[wr, wself],
        scratch=[pltpu.VMEM((2, d, d), jnp.bfloat16), pltpu.SemaphoreType.DMA((2,))],
    )


def layer_kernel(
    depth, last, in_ref, base_ref, self_ref, state_ref, src_ref, tgt_ref, asked_ref, *rest
):
    wo, wm, wn = rest[:3]
    outs, (wide, w, sems) = rest[3:-3], rest[-3:]
    after = wn if last else wn.at[depth + 1]
    copies = fetch([(wo.at[depth], w.at[0]), (wm.at[depth], w.at[1]), (after, w.at[2])], sems)
    owned, d = state_ref.shape
    incoming = unpack(in_ref, wide, d)
    v = dot(hot_rows(src_ref[...], incoming.shape[0]), incoming)
    hidden = bf(silu(v + base_ref[...].astype(jnp.float32)))
    gathered = dot(hot_columns(tgt_ref[...], owned), hidden)
    copies[0].wait()
    summed = bf(dot(bf(gathered), w[0]))
    copies[1].wait()
    update = dot(summed, w[1]) + self_ref[...]
    new = bf(state_ref[...].astype(jnp.float32) + norm(silu(update)))
    copies[2].wait()
    if last:
        outs[0][...] = bf(dot(new, w[2]))
    else:
        outs[0][...] = new
        pack(dot(new, w[2]), asked_ref, wide, outs[1])


def layer(depth, last, incoming, base, own, state, src, tgt, asked, wo, wm, wn):
    out = [(state.shape, jnp.bfloat16)]
    if not last:
        out.append((incoming.shape, jnp.bfloat16))
    d = state.shape[1]
    return on_chip(
        functools.partial(layer_kernel, depth, last),
        [incoming, base, own, state, src, tgt, asked],
        out,
        far=[wo, wm, wn],
        scratch=[
            pltpu.VMEM(incoming.shape, jnp.float32),
            pltpu.VMEM((3, d, d), jnp.bfloat16),
            pltpu.SemaphoreType.DMA((3,)),
        ],
    )


def dec_kernel(
    odd_ref, n0, n1, n2, slots_ref, wo_ref, r_ref, grid_ref, out_ref, near, slots_in, w, r, g, sems
):
    owned = n0.shape[0] // SIDE
    height = near.shape[0]
    slots = SIDE * SIDE * owned
    rows = out_ref.shape[0]
    steps = r_ref.shape[0] // rows
    step = pl.program_id(0)
    small = [
        pltpu.make_async_copy(slots_ref, slots_in, sems.at[0]),
        pltpu.make_async_copy(wo_ref, w, sems.at[1]),
    ]

    def tile(i):
        part = pl.ds(pl.multiple_of(i * rows, rows), rows)
        return (
            pltpu.make_async_copy(r_ref.at[part], r.at[part], sems.at[2 + i]),
            pltpu.make_async_copy(grid_ref.at[part], g.at[part], sems.at[2 + steps + i]),
        )

    @pl.when(step == 0)
    def _():
        for copy in small:
            copy.start()
        for i in range(steps):
            for copy in tile(i):
                copy.start()
        for k, ref in enumerate((n0, n1, n2)):
            for at in range(SIDE):
                start = pl.multiple_of(block_at(odd_ref, k * SIDE + at) * owned, 16)
                near[pl.ds(start, owned), :] = ref[at * owned : (at + 1) * owned]
        near[slots:] = jnp.zeros((height - slots, near.shape[1]), jnp.bfloat16)
        for copy in small:
            copy.wait()

    for copy in tile(step):
        copy.wait()
    part = pl.ds(pl.multiple_of(step * rows, rows), rows)
    own = r[part, :].astype(jnp.float32)
    total = None
    for f in range(DEC_FAN):
        v = dot(hot_rows(slots_in[f : f + 1, part], height), near[...]) + own
        h = bf(silu(v)).astype(jnp.float32)
        total = h if total is None else total + h
    update = dot(bf(total), w[...])
    out_ref[...] = bf(g[part, :].astype(jnp.float32) + norm(update))


def decode(odd, r, grid_latent, slot_rows, near, wo):
    n, d = r.shape
    height = up128(SIDE * near[0].shape[0])
    args = near_to(pltpu.VMEM, near) + near_to(pltpu.HBM, [slot_rows, wo, r, grid_latent])
    return pl.pallas_call(
        dec_kernel,
        grid=(n // DEC_ROWS,),
        in_specs=[pl.BlockSpec(memory_space=pltpu.SMEM)] + [VMEM] * 3 + [HBM] * 4,
        out_specs=pl.BlockSpec((DEC_ROWS, d), lambda i: (i, 0)),
        out_shape=jax.ShapeDtypeStruct((n, d), jnp.bfloat16),
        scratch_shapes=[
            pltpu.VMEM((height, d), jnp.bfloat16),
            pltpu.VMEM(slot_rows.shape, jnp.int32),
            pltpu.VMEM((d, d), jnp.bfloat16),
            pltpu.VMEM((n, d), jnp.bfloat16),
            pltpu.VMEM((n, d), jnp.bfloat16),
            pltpu.SemaphoreType.DMA((2 + 2 * (n // DEC_ROWS),)),
        ],
        compiler_params=pltpu.CompilerParams(vmem_limit_bytes=28 << 20),
        name="decode",
    )(odd, *args)


def swaps(axis):
    count = lax.axis_size(axis)
    first = [(i, i ^ 1) for i in range(count)]
    second = []
    for i in range(1, count - 1, 2):
        second += [(i, i + 1), (i + 1, i)]
    return first, second


def swap_both(axis, to_first, to_second):
    first, second = swaps(axis)
    b = lax.ppermute(to_second, axis, second)
    a = lax.ppermute(to_first, axis, first)
    return a, b


def neighbours(rows):
    a, b = swap_both("lon", rows, rows)
    line = jnp.concatenate([rows, a, b], axis=0)
    c, d = swap_both("lat", line, line)
    return line, c, d


def to_owners(sums, owned):
    a, b = swap_both("lat", sums[1], sums[2])

    def line(at):
        part = slice(at * owned, (at + 1) * owned)
        return (
            sums[0][part].astype(jnp.float32)
            + a[part].astype(jnp.float32)
            + b[part].astype(jnp.float32)
        )

    own, first, second = line(0), bf(line(1)), bf(line(2))
    c, d = swap_both("lon", first, second)
    return own, c, d


def body(
    grid_latent,
    mesh_latent,
    encoder_slots,
    decoder_slots,
    peer_rows,
    edge_source,
    edge_target,
    encoder_sender,
    encoder_receiver,
    encoder_output,
    encoder_merge,
    encoder_self,
    process_sender,
    process_receiver,
    process_output,
    process_merge,
    process_self,
    decoder_sender,
    decoder_receiver,
    decoder_output,
):
    owned = mesh_latent.shape[0]
    wanted = peer_rows[0]
    tiles = wanted.shape[0]
    odd = jnp.stack([lax.axis_index("lat") % 2, lax.axis_index("lon") % 2]).astype(jnp.int32)
    near = neighbours(mesh_latent)
    asked = lax.all_to_all(wanted, ("lat", "lon"), split_axis=0, concat_axis=0, tiled=True)
    s, e_receiver, e_slots, r = pre(
        grid_latent, encoder_sender, decoder_receiver, encoder_receiver, encoder_slots
    )
    sums = encode(odd, s, e_slots, near, e_receiver)
    own, a, b = to_owners(sums, owned)
    staged = stage(mesh_latent, encoder_output, encoder_merge, encoder_self, process_sender)
    state, outgoing = merge(own, a, b, mesh_latent, asked, staged)
    src = edge_source[None, :]
    tgt = edge_target[None, :]
    for depth in range(LAYERS):
        last = depth == LAYERS - 1
        incoming = lax.all_to_all(
            outgoing.reshape(tiles, -1, 128),
            ("lat", "lon"),
            split_axis=0,
            concat_axis=0,
            tiled=True,
        ).reshape(outgoing.shape)
        base, self_part = ready(depth, state, tgt, process_receiver, process_self)
        result = layer(
            depth,
            last,
            incoming,
            base,
            self_part,
            state,
            src,
            tgt,
            asked,
            process_output,
            process_merge,
            decoder_sender if last else process_sender,
        )
        if not last:
            state, outgoing = result
    near = neighbours(result[0])
    return decode(odd, r, grid_latent, decoder_slots, near, decoder_output)


def solution(mesh):
    return jax.shard_map(
        body,
        mesh=mesh,
        in_specs=(
            P(("lat", "lon"), None),
            P(("lat", "lon"), None),
            P(None, ("lat", "lon")),
            P(None, ("lat", "lon")),
            P(("lat", "lon"), None, None),
            P(("lat", "lon")),
            P(("lat", "lon")),
            P(),
            P(),
            P(),
            P(),
            P(),
            P(),
            P(),
            P(),
            P(),
            P(),
            P(),
            P(),
            P(),
        ),
        out_specs=P(("lat", "lon"), None),
        check_vma=False,
    )
```

```python
import functools

import jax
import jax.numpy as jnp
from jax import lax
from jax.experimental import pallas as pl
from jax.experimental.pallas import tpu as pltpu
from jax.sharding import PartitionSpec as P


LAYERS = 2
ENC_FAN = 2
DEC_FAN = 3
SIDE = 3
ENC_ROWS = 1024
DEC_ROWS = 1024
FAR_ROWS = 512
FAR_PART = 512
PRE_ROWS = 1024


def up128(n):
    return -(-n // 128) * 128


def dot(left, right):
    return jnp.dot(left, right, preferred_element_type=jnp.float32)


def silu(v):
    half = 0.5 * v
    return half + half * jnp.tanh(half)


def silu_of_half(half):
    return half + half * jnp.tanh(half)


def norm(v):
    centre = v - jnp.mean(v, axis=-1, keepdims=True)
    spread = jnp.mean(centre * centre, axis=-1, keepdims=True)
    return centre * lax.rsqrt(spread + 1e-05)


def hot_rows(row, width):
    n = row.shape[1]
    columns = jnp.broadcast_to(row, (128, n)).T
    lanes = lax.broadcasted_iota(jnp.int32, (n, 128), 1)
    parts = [
        jnp.where(lanes + at == columns, 1.0, 0.0).astype(jnp.bfloat16)
        for at in range(0, width, 128)
    ]
    return jnp.concatenate(parts, axis=1) if len(parts) > 1 else parts[0]


def hot_columns(row, height):
    subs = lax.broadcasted_iota(jnp.int32, (height, row.shape[1]), 0)
    return jnp.where(subs == row, 1.0, 0.0).astype(jnp.bfloat16)


def bf(v):
    return v.astype(jnp.bfloat16)


VMEM = pl.BlockSpec(memory_space=pltpu.VMEM)
HBM = pl.BlockSpec(memory_space=pltpu.HBM)


def near_to(space, arrays):
    return [pltpu.with_memory_space_constraint(x, space) for x in arrays]


def on_chip(kernel, args, outs, far=(), scratch=(), odd=None, limit=16):
    args = near_to(pltpu.VMEM, args)
    specs = [VMEM] * len(args) + [HBM] * len(far)
    args += near_to(pltpu.HBM, far)
    if odd is not None:
        args = [odd] + args
        specs = [pl.BlockSpec(memory_space=pltpu.SMEM)] + specs
    return pl.pallas_call(
        kernel,
        in_specs=specs,
        out_specs=[VMEM] * len(outs),
        out_shape=[pltpu.VMEM(shape, dtype) for shape, dtype in outs],
        scratch_shapes=list(scratch),
        compiler_params=pltpu.CompilerParams(vmem_limit_bytes=limit << 20),
    )(*args)


def fetch(pairs, sems):
    copies = [pltpu.make_async_copy(x, y, sems.at[i]) for i, (x, y) in enumerate(pairs)]
    for copy in copies:
        copy.start()
    return copies


def receiver_kernel(grid_ref, w_ref, r_ref):
    r_ref[...] = bf(dot(grid_ref[...], w_ref[...] * jnp.bfloat16(0.5)))


def receiver(grid_latent, w):
    n, d = grid_latent.shape
    tile = pl.BlockSpec((PRE_ROWS, d), lambda i: (i, 0))
    return pl.pallas_call(
        receiver_kernel,
        grid=(n // PRE_ROWS,),
        in_specs=[tile, pl.BlockSpec((d, d), lambda i: (0, 0))],
        out_specs=tile,
        out_shape=pltpu.HBM((n, d), jnp.bfloat16),
        compiler_params=pltpu.CompilerParams(vmem_limit_bytes=16 << 20),
        name="receiver",
    )(*near_to(pltpu.HBM, [grid_latent, w]))


def line_rows(rows, near, start, odd_ref):
    owned = rows.shape[0] // SIDE
    odd = odd_ref[1]
    for at, spot in enumerate((1, 2 - 2 * odd, 2 * odd)):
        to = pl.multiple_of(start + spot * owned, 16)
        near[pl.ds(to, owned), :] = rows[at * owned : (at + 1) * owned]


def line_start(place, odd_ref, line):
    odd = odd_ref[0]
    return (1, 2 - 2 * odd, 2 * odd)[place] * line


def up256(n):
    return -(-n // 256) * 256


def block_at(odd_ref, place):
    spots = []
    for axis, at in enumerate((place // SIDE, place % SIDE)):
        odd = odd_ref[axis]
        spots.append((1, 2 - 2 * odd, 2 * odd)[at])
    return spots[0] * SIDE + spots[1]


def enc_near_kernel(
    odd_ref, n0, n1, slots_ref, wr_ref, ws_ref, grid_ref, v_ref, slots, wr, near, ws, g, sems
):
    line = n0.shape[0]
    wide = near.shape[0] // 2
    rows = ENC_ROWS
    parts = [slice(i, i + rows) for i in range(0, g.shape[0], rows)]
    pairs = [(wr_ref, wr), (ws_ref, ws), (slots_ref, slots)]
    pairs += [(grid_ref.at[part], g.at[part]) for part in parts]
    copies = fetch(pairs, sems)
    near[...] = jnp.zeros_like(near)
    copies[0].wait()
    for k, ref in enumerate((n0, n1)):
        line_rows(bf(dot(ref[...], wr[...]) * 0.5), near, k * wide, odd_ref)
    copies[1].wait()
    copies[2].wait()
    for i, part in enumerate(parts):
        copies[3 + i].wait()
        s = dot(g[part], ws[...]) * 0.5
        for f in range(ENC_FAN):
            slot = slots[f : f + 1, part]
            chosen = jnp.concatenate(
                [hot_rows(slot - line_start(k, odd_ref, line), wide) for k in range(2)], axis=1
            )
            v_ref[f, part] = dot(chosen, near[...]) + s


def encode_near(odd, grid_latent, slot_rows, near, wr, ws):
    n, d = grid_latent.shape
    return on_chip(
        enc_near_kernel,
        list(near),
        [
            ((ENC_FAN, n, d), jnp.float32),
            (slot_rows.shape, jnp.int32),
            ((d, d), jnp.bfloat16),
        ],
        far=[slot_rows, wr, ws, grid_latent],
        scratch=[
            pltpu.VMEM((2 * up256(near[0].shape[0]), d), jnp.bfloat16),
            pltpu.VMEM((d, d), jnp.bfloat16),
            pltpu.VMEM((n, d), jnp.bfloat16),
            pltpu.SemaphoreType.DMA((3 + n // ENC_ROWS,)),
        ],
        odd=odd,
    )


def enc_far_kernel(odd_ref, n2, v_ref, slots_ref, wr_ref, o0, o1, o2, near, acc, hid):
    line = n2.shape[0]
    owned = line // SIDE
    slots = SIDE * line
    rows = hid.shape[0] // ENC_FAN

    near[...] = jnp.zeros_like(near)
    line_rows(bf(dot(n2[...], wr_ref[...]) * 0.5), near, 0, odd_ref)
    start = line_start(2, odd_ref, line)
    for step in range(v_ref.shape[1] // rows):
        part = slice(step * rows, (step + 1) * rows)
        for f in range(ENC_FAN):
            chosen = hot_rows(slots_ref[f : f + 1, part] - start, near.shape[0])
            v = dot(chosen, near[...]) + v_ref[f, part]
            hid[f * rows : (f + 1) * rows] = bf(silu_of_half(v))
        chosen = jnp.concatenate(
            [hot_columns(slots_ref[f : f + 1, part], slots) for f in range(ENC_FAN)], axis=1
        )
        sums = dot(chosen, hid[...])
        acc[...] = sums if step == 0 else acc[...] + sums

    for k, ref in enumerate((o0, o1, o2)):
        for at in range(SIDE):
            first = pl.multiple_of(block_at(odd_ref, k * SIDE + at) * owned, 16)
            ref[at * owned : (at + 1) * owned] = bf(acc[pl.ds(first, owned), :])


def encode_far(odd, near, prepared):
    v, slots, wr = prepared
    line, d = near.shape
    return on_chip(
        enc_far_kernel,
        [near, v, slots, wr],
        [((line, d), jnp.bfloat16)] * SIDE,
        scratch=[
            pltpu.VMEM((up256(line), d), jnp.bfloat16),
            pltpu.VMEM((SIDE * line, d), jnp.float32),
            pltpu.VMEM((ENC_FAN * ENC_ROWS, d), jnp.bfloat16),
        ],
        odd=odd,
    )


def pack(sent, asked_ref, wide, out_ref):
    sent = padded_rows(bf(sent))
    tiles, cap = asked_ref.shape
    parts = sent.shape[1] // 128
    lanes = lax.broadcasted_iota(jnp.int32, (tiles, sent.shape[0]), 1)
    for k in range(cap):
        chosen = bf(jnp.where(lanes == asked_ref[:, k : k + 1], 1.0, 0.0))
        rows = dot(chosen, sent)
        for c in range(parts):
            wide[pl.ds(k * parts + c, tiles, stride=cap * parts), :] = rows[
                :, c * 128 : (c + 1) * 128
            ]
    out_ref[...] = bf(wide[...])


def unpack(in_ref, wide, d):
    parts = d // 128
    n = in_ref.shape[0] // parts
    wide[...] = in_ref[...].astype(jnp.float32)
    return jnp.concatenate(
        [bf(wide[pl.ds(c, n, stride=parts), :]) for c in range(parts)], axis=1
    )


def padded_rows(rows):
    extra = up128(rows.shape[0]) - rows.shape[0]
    return jnp.concatenate([rows, jnp.zeros((extra, rows.shape[1]), rows.dtype)], axis=0)


def stage_kernel(mesh, wo, wm, wself, ws, wo_out, wm_out, ws_out, self_ref, w, sems):
    copies = fetch([(wself, w), (wo, wo_out), (wm, wm_out), (ws.at[0], ws_out)], sems)
    copies[0].wait()
    self_ref[...] = dot(mesh[...], w[...])
    for copy in copies[1:]:
        copy.wait()


def stage(mesh, wo, wm, wself, ws):
    rows, d = mesh.shape
    return on_chip(
        stage_kernel,
        [mesh],
        [((d, d), jnp.bfloat16)] * 3 + [((rows, d), jnp.float32)],
        far=[wo, wm, wself, ws],
        scratch=[pltpu.VMEM((d, d), jnp.bfloat16), pltpu.SemaphoreType.DMA((4,))],
    )


def merge_kernel(
    o_ref, a_ref, b_ref, mesh_ref, asked_ref, wo, wm, ws, self_ref, state_ref, out_ref, wide
):
    total = o_ref[...] + a_ref[...].astype(jnp.float32) + b_ref[...].astype(jnp.float32)
    summed = bf(dot(bf(total), wo[...]))
    update = dot(summed, wm[...]) + self_ref[...]
    state = bf(mesh_ref[...].astype(jnp.float32) + norm(silu(update)))
    state_ref[...] = state
    pack(dot(state, ws[...]), asked_ref, wide, out_ref)


def merge(own, a, b, mesh, asked, staged):
    packed = (asked.size * mesh.shape[1] // 128, 128)
    return on_chip(
        merge_kernel,
        [own, a, b, mesh, asked, *staged],
        [(mesh.shape, jnp.bfloat16), (packed, jnp.bfloat16)],
        scratch=[pltpu.VMEM(packed, jnp.float32)],
    )


def ready_kernel(depth, state_ref, tgt_ref, wr, wself, base_ref, self_ref, w, sems):
    copies = fetch([(wr.at[depth], w.at[0]), (wself.at[depth], w.at[1])], sems)
    state = state_ref[...]
    chosen = hot_rows(tgt_ref[...], up128(state.shape[0]))
    copies[0].wait()
    received = padded_rows(bf(dot(state, w[0])))
    base_ref[...] = bf(dot(chosen, received))
    copies[1].wait()
    self_ref[...] = dot(state, w[1])


def ready(depth, state, tgt, wr, wself):
    rows, d = state.shape
    return on_chip(
        functools.partial(ready_kernel, depth),
        [state, tgt],
        [((tgt.shape[1], d), jnp.bfloat16), ((rows, d), jnp.float32)],
        far=[wr, wself],
        scratch=[pltpu.VMEM((2, d, d), jnp.bfloat16), pltpu.SemaphoreType.DMA((2,))],
    )


def layer_kernel(
    depth, last, in_ref, base_ref, self_ref, state_ref, src_ref, tgt_ref, asked_ref, *rest
):
    wo, wm, wn = rest[:3]
    outs, (wide, w, sems) = rest[3:-3], rest[-3:]
    after = wn if last else wn.at[depth + 1]
    copies = fetch([(wo.at[depth], w.at[0]), (wm.at[depth], w.at[1]), (after, w.at[2])], sems)
    owned, d = state_ref.shape
    incoming = unpack(in_ref, wide, d)
    v = dot(hot_rows(src_ref[...], incoming.shape[0]), incoming)
    hidden = bf(silu(v + base_ref[...].astype(jnp.float32)))
    gathered = dot(hot_columns(tgt_ref[...], owned), hidden)
    copies[0].wait()
    summed = bf(dot(bf(gathered), w[0]))
    copies[1].wait()
    update = dot(summed, w[1]) + self_ref[...]
    new = bf(state_ref[...].astype(jnp.float32) + norm(silu(update)))
    copies[2].wait()
    if last:
        outs[0][...] = bf(dot(new, w[2]) * 0.5)
    else:
        outs[0][...] = new
        pack(dot(new, w[2]), asked_ref, wide, outs[1])


def layer(depth, last, incoming, base, own, state, src, tgt, asked, wo, wm, wn):
    out = [(state.shape, jnp.bfloat16)]
    if not last:
        out.append((incoming.shape, jnp.bfloat16))
    d = state.shape[1]
    return on_chip(
        functools.partial(layer_kernel, depth, last),
        [incoming, base, own, state, src, tgt, asked],
        out,
        far=[wo, wm, wn],
        scratch=[
            pltpu.VMEM(incoming.shape, jnp.float32),
            pltpu.VMEM((3, d, d), jnp.bfloat16),
            pltpu.SemaphoreType.DMA((3,)),
        ],
    )


def dec_near_kernel(
    odd_ref, n0, n1, slots_ref, wo_ref, grid_ref, r_ref, v_ref, slots, w, g, near, r, sems
):
    line = n0.shape[0]
    wide = near.shape[0] // 2
    rows = DEC_ROWS
    parts = [slice(i, i + rows) for i in range(0, r_ref.shape[0], rows)]
    pairs = [(slots_ref, slots)] + [(r_ref.at[part], r.at[part]) for part in parts]
    pairs += [(wo_ref, w), (grid_ref, g)]
    copies = fetch(pairs, sems)
    near[...] = jnp.zeros_like(near)
    for k, ref in enumerate((n0, n1)):
        line_rows(ref[...], near, k * wide, odd_ref)
    copies[0].wait()
    for i, part in enumerate(parts):
        copies[1 + i].wait()
        own = r[part].astype(jnp.float32)
        for f in range(DEC_FAN):
            slot = slots[f : f + 1, part]
            chosen = jnp.concatenate(
                [hot_rows(slot - line_start(k, odd_ref, line), wide) for k in range(2)], axis=1
            )
            v_ref[f, part] = dot(chosen, near[...]) + own
    for copy in copies[1 + len(parts) :]:
        copy.wait()


def dec_far_kernel(odd_ref, n2, v, slots, w, g, out_ref, near):
    line = n2.shape[0]
    rows = out_ref.shape[0]
    step = pl.program_id(0)

    @pl.when(step == 0)
    def _():
        near[...] = jnp.zeros_like(near)
        line_rows(n2[...], near, 0, odd_ref)

    start = line_start(2, odd_ref, line)
    for at in range(0, rows, FAR_PART):
        part = pl.ds(pl.multiple_of(step * rows + at, FAR_PART), FAR_PART)
        total = None
        for f in range(DEC_FAN):
            chosen = hot_rows(slots[f : f + 1, part] - start, near.shape[0])
            h = silu_of_half(dot(chosen, near[...]) + v[f, part, :])
            total = h if total is None else total + h
        update = dot(bf(total), w[...])
        out_ref[at : at + FAR_PART] = bf(g[part, :].astype(jnp.float32) + norm(update))


def decode_near(odd, r, grid_latent, slot_rows, near, wo):
    n, d = r.shape
    wide = up256(near[0].shape[0])
    return on_chip(
        dec_near_kernel,
        list(near),
        [
            ((DEC_FAN, n, d), jnp.float32),
            (slot_rows.shape, jnp.int32),
            (wo.shape, jnp.bfloat16),
            ((n, d), jnp.bfloat16),
        ],
        far=[slot_rows, wo, grid_latent, r],
        scratch=[
            pltpu.VMEM((2 * wide, d), jnp.bfloat16),
            pltpu.VMEM((n, d), jnp.bfloat16),
            pltpu.SemaphoreType.DMA((3 + n // DEC_ROWS,)),
        ],
        odd=odd,
        limit=16,
    )


def decode_far(odd, near, prepared):
    v, slots, w, g = prepared
    n, d = g.shape
    args = near_to(pltpu.VMEM, [near, v, slots, w, g])
    return pl.pallas_call(
        dec_far_kernel,
        grid=(n // FAR_ROWS,),
        in_specs=[pl.BlockSpec(memory_space=pltpu.SMEM)] + [VMEM] * len(args),
        out_specs=pl.BlockSpec((FAR_ROWS, d), lambda i: (i, 0)),
        out_shape=jax.ShapeDtypeStruct((n, d), jnp.bfloat16),
        scratch_shapes=[pltpu.VMEM((up256(near.shape[0]), d), jnp.bfloat16)],
        compiler_params=pltpu.CompilerParams(vmem_limit_bytes=20 << 20),
        name="decode_far",
    )(odd, *args)


def swaps(axis):
    count = lax.axis_size(axis)
    first = [(i, i ^ 1) for i in range(count)]
    second = []
    for i in range(1, count - 1, 2):
        second += [(i, i + 1), (i + 1, i)]
    return first, second


def swap_both(axis, to_first, to_second):
    first, second = swaps(axis)
    b = lax.ppermute(to_second, axis, second)
    a = lax.ppermute(to_first, axis, first)
    return a, b


def neighbours(rows):
    a, b = swap_both("lon", rows, rows)
    line = jnp.concatenate([rows, a, b], axis=0)
    c, d = swap_both("lat", line, line)
    return line, c, d


def to_owners(sums, owned):
    a, b = swap_both("lat", sums[1], sums[2])

    def line(at):
        part = slice(at * owned, (at + 1) * owned)
        return (
            sums[0][part].astype(jnp.float32)
            + a[part].astype(jnp.float32)
            + b[part].astype(jnp.float32)
        )

    own, first, second = line(0), bf(line(1)), bf(line(2))
    c, d = swap_both("lon", first, second)
    return own, c, d


def body(
    grid_latent,
    mesh_latent,
    encoder_slots,
    decoder_slots,
    peer_rows,
    edge_source,
    edge_target,
    encoder_sender,
    encoder_receiver,
    encoder_output,
    encoder_merge,
    encoder_self,
    process_sender,
    process_receiver,
    process_output,
    process_merge,
    process_self,
    decoder_sender,
    decoder_receiver,
    decoder_output,
):
    owned = mesh_latent.shape[0]
    wanted = peer_rows[0]
    tiles = wanted.shape[0]
    odd = jnp.stack([lax.axis_index("lat") % 2, lax.axis_index("lon") % 2]).astype(jnp.int32)
    near = neighbours(mesh_latent)
    asked = lax.all_to_all(wanted, ("lat", "lon"), split_axis=0, concat_axis=0, tiled=True)
    prepared = encode_near(
        odd, grid_latent, encoder_slots, near[:2], encoder_receiver, encoder_sender
    )
    sums = encode_far(odd, near[2], prepared)
    own, a, b = to_owners(sums, owned)
    staged = stage(mesh_latent, encoder_output, encoder_merge, encoder_self, process_sender)
    state, outgoing = merge(own, a, b, mesh_latent, asked, staged)
    r = receiver(grid_latent, decoder_receiver)
    src = edge_source[None, :]
    tgt = edge_target[None, :]
    for depth in range(LAYERS):
        last = depth == LAYERS - 1
        incoming = lax.all_to_all(
            outgoing.reshape(tiles, -1, 128),
            ("lat", "lon"),
            split_axis=0,
            concat_axis=0,
            tiled=True,
        ).reshape(outgoing.shape)
        base, self_part = ready(depth, state, tgt, process_receiver, process_self)
        result = layer(
            depth,
            last,
            incoming,
            base,
            self_part,
            state,
            src,
            tgt,
            asked,
            process_output,
            process_merge,
            decoder_sender if last else process_sender,
        )
        if not last:
            state, outgoing = result
    near = neighbours(result[0])
    prepared = decode_near(odd, r, grid_latent, decoder_slots, near[:2], decoder_output)
    return decode_far(odd, near[2], prepared)


def solution(mesh):
    return jax.shard_map(
        body,
        mesh=mesh,
        in_specs=(
            P(("lat", "lon"), None),
            P(("lat", "lon"), None),
            P(None, ("lat", "lon")),
            P(None, ("lat", "lon")),
            P(("lat", "lon"), None, None),
            P(("lat", "lon")),
            P(("lat", "lon")),
            P(),
            P(),
            P(),
            P(),
            P(),
            P(),
            P(),
            P(),
            P(),
            P(),
            P(),
            P(),
            P(),
        ),
        out_specs=P(("lat", "lon"), None),
        check_vma=False,
    )
```

```python
import functools

import jax
import jax.numpy as jnp
from jax import lax
from jax.experimental import pallas as pl
from jax.experimental.pallas import tpu as pltpu
from jax.sharding import PartitionSpec as P


LAYERS = 2
ENC_FAN = 2
DEC_FAN = 3
SIDE = 3
ENC_ROWS = 1024
DEC_ROWS = 1024
FAR_ROWS = 512
FAR_PART = 512
PRE_ROWS = 1024


def up128(n):
    return -(-n // 128) * 128


def dot(left, right):
    return jnp.dot(left, right, preferred_element_type=jnp.float32)


def silu(v):
    half = 0.5 * v
    return half + half * jnp.tanh(half)


def silu_of_half(half):
    half = bf(half)
    return half + half * jnp.tanh(half)


def norm(v):
    centre = v - jnp.mean(v, axis=-1, keepdims=True)
    spread = jnp.mean(centre * centre, axis=-1, keepdims=True)
    return centre * lax.rsqrt(spread + 1e-05)


def hot_rows(row, width):
    n = row.shape[1]
    columns = jnp.broadcast_to(row, (128, n)).T
    lanes = lax.broadcasted_iota(jnp.int32, (n, 128), 1)
    parts = [
        jnp.where(lanes + at == columns, 1.0, 0.0).astype(jnp.bfloat16)
        for at in range(0, width, 128)
    ]
    return jnp.concatenate(parts, axis=1) if len(parts) > 1 else parts[0]


def hot_columns(row, height):
    subs = lax.broadcasted_iota(jnp.int32, (height, row.shape[1]), 0)
    return jnp.where(subs == row, 1.0, 0.0).astype(jnp.bfloat16)


def bf(v):
    return v.astype(jnp.bfloat16)


VMEM = pl.BlockSpec(memory_space=pltpu.VMEM)
HBM = pl.BlockSpec(memory_space=pltpu.HBM)


def near_to(space, arrays):
    return [pltpu.with_memory_space_constraint(x, space) for x in arrays]


def on_chip(kernel, args, outs, far=(), scratch=(), odd=None, limit=16):
    args = near_to(pltpu.VMEM, args)
    specs = [VMEM] * len(args) + [HBM] * len(far)
    args += near_to(pltpu.HBM, far)
    if odd is not None:
        args = [odd] + args
        specs = [pl.BlockSpec(memory_space=pltpu.SMEM)] + specs
    return pl.pallas_call(
        kernel,
        in_specs=specs,
        out_specs=[VMEM] * len(outs),
        out_shape=[pltpu.VMEM(shape, dtype) for shape, dtype in outs],
        scratch_shapes=list(scratch),
        compiler_params=pltpu.CompilerParams(vmem_limit_bytes=limit << 20),
    )(*args)


def fetch(pairs, sems):
    copies = [pltpu.make_async_copy(x, y, sems.at[i]) for i, (x, y) in enumerate(pairs)]
    for copy in copies:
        copy.start()
    return copies


def receiver_kernel(grid_ref, w_ref, r_ref):
    r_ref[...] = bf(dot(grid_ref[...], w_ref[...] * jnp.bfloat16(0.5)))


def receiver(grid_latent, w):
    n, d = grid_latent.shape
    tile = pl.BlockSpec((PRE_ROWS, d), lambda i: (i, 0))
    return pl.pallas_call(
        receiver_kernel,
        grid=(n // PRE_ROWS,),
        in_specs=[tile, pl.BlockSpec((d, d), lambda i: (0, 0))],
        out_specs=tile,
        out_shape=pltpu.HBM((n, d), jnp.bfloat16),
        compiler_params=pltpu.CompilerParams(vmem_limit_bytes=16 << 20),
        name="receiver",
    )(*near_to(pltpu.HBM, [grid_latent, w]))


def line_rows(rows, near, start, odd_ref):
    owned = rows.shape[0] // SIDE
    odd = odd_ref[1]
    for at, spot in enumerate((1, 2 - 2 * odd, 2 * odd)):
        to = pl.multiple_of(start + spot * owned, 16)
        near[pl.ds(to, owned), :] = rows[at * owned : (at + 1) * owned]


def line_start(place, odd_ref, line):
    odd = odd_ref[0]
    return (1, 2 - 2 * odd, 2 * odd)[place] * line


def up256(n):
    return -(-n // 256) * 256


def block_at(odd_ref, place):
    spots = []
    for axis, at in enumerate((place // SIDE, place % SIDE)):
        odd = odd_ref[axis]
        spots.append((1, 2 - 2 * odd, 2 * odd)[at])
    return spots[0] * SIDE + spots[1]


def enc_near_kernel(
    odd_ref, n0, n1, slots_ref, wr_ref, ws_ref, grid_ref, v_ref, slots, wr, near, ws, g, sems
):
    line = n0.shape[0]
    wide = near.shape[0] // 2
    rows = ENC_ROWS
    parts = [slice(i, i + rows) for i in range(0, g.shape[0], rows)]
    pairs = [(wr_ref, wr), (ws_ref, ws), (slots_ref, slots)]
    pairs += [(grid_ref.at[part], g.at[part]) for part in parts]
    copies = fetch(pairs, sems)
    near[...] = jnp.zeros_like(near)
    copies[0].wait()
    for k, ref in enumerate((n0, n1)):
        line_rows(bf(dot(ref[...], wr[...]) * 0.5), near, k * wide, odd_ref)
    copies[1].wait()
    copies[2].wait()
    for i, part in enumerate(parts):
        copies[3 + i].wait()
        s = dot(g[part], ws[...]) * 0.5
        for f in range(ENC_FAN):
            slot = slots[f : f + 1, part]
            chosen = jnp.concatenate(
                [hot_rows(slot - line_start(k, odd_ref, line), wide) for k in range(2)], axis=1
            )
            v_ref[f, part] = dot(chosen, near[...]) + s


def encode_near(odd, grid_latent, slot_rows, near, wr, ws):
    n, d = grid_latent.shape
    return on_chip(
        enc_near_kernel,
        list(near),
        [
            ((ENC_FAN, n, d), jnp.float32),
            (slot_rows.shape, jnp.int32),
            ((d, d), jnp.bfloat16),
        ],
        far=[slot_rows, wr, ws, grid_latent],
        scratch=[
            pltpu.VMEM((2 * up256(near[0].shape[0]), d), jnp.bfloat16),
            pltpu.VMEM((d, d), jnp.bfloat16),
            pltpu.VMEM((n, d), jnp.bfloat16),
            pltpu.SemaphoreType.DMA((3 + n // ENC_ROWS,)),
        ],
        odd=odd,
    )


def enc_far_kernel(odd_ref, n2, v_ref, slots_ref, wr_ref, o0, o1, o2, near, acc, hid):
    line = n2.shape[0]
    owned = line // SIDE
    slots = SIDE * line
    rows = hid.shape[0] // ENC_FAN

    near[...] = jnp.zeros_like(near)
    line_rows(bf(dot(n2[...], wr_ref[...]) * 0.5), near, 0, odd_ref)
    start = line_start(2, odd_ref, line)
    for step in range(v_ref.shape[1] // rows):
        part = slice(step * rows, (step + 1) * rows)
        for f in range(ENC_FAN):
            chosen = hot_rows(slots_ref[f : f + 1, part] - start, near.shape[0])
            v = dot(chosen, near[...]) + v_ref[f, part]
            hid[f * rows : (f + 1) * rows] = silu_of_half(v)
        chosen = jnp.concatenate(
            [hot_columns(slots_ref[f : f + 1, part], slots) for f in range(ENC_FAN)], axis=1
        )
        sums = dot(chosen, hid[...])
        acc[...] = sums if step == 0 else acc[...] + sums

    for k, ref in enumerate((o0, o1, o2)):
        for at in range(SIDE):
            first = pl.multiple_of(block_at(odd_ref, k * SIDE + at) * owned, 16)
            ref[at * owned : (at + 1) * owned] = bf(acc[pl.ds(first, owned), :])


def encode_far(odd, near, prepared):
    v, slots, wr = prepared
    line, d = near.shape
    return on_chip(
        enc_far_kernel,
        [near, v, slots, wr],
        [((line, d), jnp.bfloat16)] * SIDE,
        scratch=[
            pltpu.VMEM((up256(line), d), jnp.bfloat16),
            pltpu.VMEM((SIDE * line, d), jnp.float32),
            pltpu.VMEM((ENC_FAN * ENC_ROWS, d), jnp.bfloat16),
        ],
        odd=odd,
    )


def pack(sent, asked_ref, wide, out_ref):
    sent = padded_rows(bf(sent))
    tiles, cap = asked_ref.shape
    parts = sent.shape[1] // 128
    lanes = lax.broadcasted_iota(jnp.int32, (tiles, sent.shape[0]), 1)
    for k in range(cap):
        chosen = bf(jnp.where(lanes == asked_ref[:, k : k + 1], 1.0, 0.0))
        rows = dot(chosen, sent)
        for c in range(parts):
            wide[pl.ds(k * parts + c, tiles, stride=cap * parts), :] = rows[
                :, c * 128 : (c + 1) * 128
            ]
    out_ref[...] = bf(wide[...])


def unpack(in_ref, wide, d):
    parts = d // 128
    n = in_ref.shape[0] // parts
    wide[...] = in_ref[...].astype(jnp.float32)
    return jnp.concatenate(
        [bf(wide[pl.ds(c, n, stride=parts), :]) for c in range(parts)], axis=1
    )


def padded_rows(rows):
    extra = up128(rows.shape[0]) - rows.shape[0]
    return jnp.concatenate([rows, jnp.zeros((extra, rows.shape[1]), rows.dtype)], axis=0)


def stage_kernel(mesh, wo, wm, wself, ws, wom_out, ws_out, self_ref, w, sems):
    copies = fetch([(wself, w.at[0]), (wo, w.at[1]), (wm, w.at[2]), (ws.at[0], ws_out)], sems)
    copies[0].wait()
    self_ref[...] = dot(mesh[...], w[0])
    copies[1].wait()
    copies[2].wait()
    wom_out[...] = bf(dot(w[1], w[2]))
    copies[3].wait()


def stage(mesh, wo, wm, wself, ws):
    rows, d = mesh.shape
    return on_chip(
        stage_kernel,
        [mesh],
        [((d, d), jnp.bfloat16)] * 2 + [((rows, d), jnp.float32)],
        far=[wo, wm, wself, ws],
        scratch=[pltpu.VMEM((3, d, d), jnp.bfloat16), pltpu.SemaphoreType.DMA((4,))],
    )


def merge_kernel(
    o_ref, a_ref, b_ref, mesh_ref, asked_ref, wom, ws, self_ref, state_ref, out_ref, wide
):
    total = o_ref[...] + a_ref[...].astype(jnp.float32) + b_ref[...].astype(jnp.float32)
    update = dot(bf(total), wom[...]) + self_ref[...]
    state = bf(mesh_ref[...].astype(jnp.float32) + norm(silu(update)))
    state_ref[...] = state
    pack(dot(state, ws[...]), asked_ref, wide, out_ref)


def merge(own, a, b, mesh, asked, staged):
    packed = (asked.size * mesh.shape[1] // 128, 128)
    return on_chip(
        merge_kernel,
        [own, a, b, mesh, asked, *staged],
        [(mesh.shape, jnp.bfloat16), (packed, jnp.bfloat16)],
        scratch=[pltpu.VMEM(packed, jnp.float32)],
    )


def ready_kernel(
    depth, last, state_ref, tgt_ref, wr, wself, wo, wm, wn, base_ref, self_ref, wom, wn_out, w, sems
):
    pairs = [(x.at[depth], w.at[i]) for i, x in enumerate((wr, wself, wo, wm))]
    copies = fetch(pairs + [(wn if last else wn.at[depth + 1], wn_out)], sems)
    state = state_ref[...]
    chosen = hot_rows(tgt_ref[...], up128(state.shape[0]))
    copies[0].wait()
    received = padded_rows(bf(dot(state, w[0])))
    base_ref[...] = bf(dot(chosen, received))
    copies[1].wait()
    self_ref[...] = dot(state, w[1])
    copies[2].wait()
    copies[3].wait()
    wom[...] = bf(dot(w[2], w[3]))
    copies[4].wait()


def ready(depth, last, state, tgt, wr, wself, wo, wm, wn):
    rows, d = state.shape
    return on_chip(
        functools.partial(ready_kernel, depth, last),
        [state, tgt],
        [((tgt.shape[1], d), jnp.bfloat16), ((rows, d), jnp.float32)]
        + [((d, d), jnp.bfloat16)] * 2,
        far=[wr, wself, wo, wm, wn],
        scratch=[pltpu.VMEM((4, d, d), jnp.bfloat16), pltpu.SemaphoreType.DMA((5,))],
    )


def layer_kernel(
    last, in_ref, base_ref, self_ref, wom, wn, state_ref, src_ref, tgt_ref, asked_ref, *rest
):
    outs, wide = rest[:-1], rest[-1]
    owned, d = state_ref.shape
    incoming = unpack(in_ref, wide, d)
    v = dot(hot_rows(src_ref[...], incoming.shape[0]), incoming)
    hidden = bf(silu(v + base_ref[...].astype(jnp.float32)))
    gathered = dot(hot_columns(tgt_ref[...], owned), hidden)
    update = dot(bf(gathered), wom[...]) + self_ref[...]
    new = bf(state_ref[...].astype(jnp.float32) + norm(silu(update)))
    if last:
        outs[0][...] = bf(dot(new, wn[...]) * 0.5)
    else:
        outs[0][...] = new
        pack(dot(new, wn[...]), asked_ref, wide, outs[1])


def layer(last, incoming, prepared, state, src, tgt, asked):
    out = [(state.shape, jnp.bfloat16)]
    if not last:
        out.append((incoming.shape, jnp.bfloat16))
    return on_chip(
        functools.partial(layer_kernel, last),
        [incoming, *prepared, state, src, tgt, asked],
        out,
        scratch=[pltpu.VMEM(incoming.shape, jnp.float32)],
    )


def dec_near_kernel(
    odd_ref, n0, n1, slots_ref, wo_ref, grid_ref, r_ref, v_ref, slots, w, g, near, r, sems
):
    line = n0.shape[0]
    wide = near.shape[0] // 2
    rows = DEC_ROWS
    parts = [slice(i, i + rows) for i in range(0, r_ref.shape[0], rows)]
    pairs = [(slots_ref, slots)] + [(r_ref.at[part], r.at[part]) for part in parts]
    pairs += [(wo_ref, w), (grid_ref, g)]
    copies = fetch(pairs, sems)
    near[...] = jnp.zeros_like(near)
    for k, ref in enumerate((n0, n1)):
        line_rows(ref[...], near, k * wide, odd_ref)
    copies[0].wait()
    for i, part in enumerate(parts):
        copies[1 + i].wait()
        own = r[part].astype(jnp.float32)
        for f in range(DEC_FAN):
            slot = slots[f : f + 1, part]
            chosen = jnp.concatenate(
                [hot_rows(slot - line_start(k, odd_ref, line), wide) for k in range(2)], axis=1
            )
            v_ref[f, part] = dot(chosen, near[...]) + own
    for copy in copies[1 + len(parts) :]:
        copy.wait()


def dec_far_kernel(odd_ref, n2, v, slots, w, g, out_ref, near):
    line = n2.shape[0]
    rows = out_ref.shape[0]
    step = pl.program_id(0)

    @pl.when(step == 0)
    def _():
        near[...] = jnp.zeros_like(near)
        line_rows(n2[...], near, 0, odd_ref)

    start = line_start(2, odd_ref, line)
    for at in range(0, rows, FAR_PART):
        part = pl.ds(pl.multiple_of(step * rows + at, FAR_PART), FAR_PART)
        total = None
        for f in range(DEC_FAN):
            chosen = hot_rows(slots[f : f + 1, part] - start, near.shape[0])
            h = silu_of_half(dot(chosen, near[...]) + v[f, part, :]).astype(jnp.float32)
            total = h if total is None else total + h
        update = dot(bf(total), w[...])
        out_ref[at : at + FAR_PART] = bf(g[part, :].astype(jnp.float32) + norm(update))


def decode_near(odd, r, grid_latent, slot_rows, near, wo):
    n, d = r.shape
    wide = up256(near[0].shape[0])
    return on_chip(
        dec_near_kernel,
        list(near),
        [
            ((DEC_FAN, n, d), jnp.float32),
            (slot_rows.shape, jnp.int32),
            (wo.shape, jnp.bfloat16),
            ((n, d), jnp.bfloat16),
        ],
        far=[slot_rows, wo, grid_latent, r],
        scratch=[
            pltpu.VMEM((2 * wide, d), jnp.bfloat16),
            pltpu.VMEM((n, d), jnp.bfloat16),
            pltpu.SemaphoreType.DMA((3 + n // DEC_ROWS,)),
        ],
        odd=odd,
        limit=16,
    )


def decode_far(odd, near, prepared):
    v, slots, w, g = prepared
    n, d = g.shape
    args = near_to(pltpu.VMEM, [near, v, slots, w, g])
    return pl.pallas_call(
        dec_far_kernel,
        grid=(n // FAR_ROWS,),
        in_specs=[pl.BlockSpec(memory_space=pltpu.SMEM)] + [VMEM] * len(args),
        out_specs=pl.BlockSpec((FAR_ROWS, d), lambda i: (i, 0)),
        out_shape=jax.ShapeDtypeStruct((n, d), jnp.bfloat16),
        scratch_shapes=[pltpu.VMEM((up256(near.shape[0]), d), jnp.bfloat16)],
        compiler_params=pltpu.CompilerParams(vmem_limit_bytes=20 << 20),
        name="decode_far",
    )(odd, *args)


def swaps(axis):
    count = lax.axis_size(axis)
    first = [(i, i ^ 1) for i in range(count)]
    second = []
    for i in range(1, count - 1, 2):
        second += [(i, i + 1), (i + 1, i)]
    return first, second


def swap_both(axis, to_first, to_second):
    first, second = swaps(axis)
    b = lax.ppermute(to_second, axis, second)
    a = lax.ppermute(to_first, axis, first)
    return a, b


def neighbours(rows):
    a, b = swap_both("lon", rows, rows)
    line = jnp.concatenate([rows, a, b], axis=0)
    c, d = swap_both("lat", line, line)
    return line, c, d


def to_owners(sums, owned):
    a, b = swap_both("lat", sums[1], sums[2])

    def line(at):
        part = slice(at * owned, (at + 1) * owned)
        return (
            sums[0][part].astype(jnp.float32)
            + a[part].astype(jnp.float32)
            + b[part].astype(jnp.float32)
        )

    own, first, second = line(0), bf(line(1)), bf(line(2))
    c, d = swap_both("lon", first, second)
    return own, c, d


def body(
    grid_latent,
    mesh_latent,
    encoder_slots,
    decoder_slots,
    peer_rows,
    edge_source,
    edge_target,
    encoder_sender,
    encoder_receiver,
    encoder_output,
    encoder_merge,
    encoder_self,
    process_sender,
    process_receiver,
    process_output,
    process_merge,
    process_self,
    decoder_sender,
    decoder_receiver,
    decoder_output,
):
    owned = mesh_latent.shape[0]
    tiles = peer_rows.shape[1]
    odd = jnp.stack([lax.axis_index("lat") % 2, lax.axis_index("lon") % 2]).astype(jnp.int32)
    near = neighbours(mesh_latent)
    prepared = encode_near(
        odd, grid_latent, encoder_slots, near[:2], encoder_receiver, encoder_sender
    )
    asked = lax.all_to_all(peer_rows[0], ("lat", "lon"), split_axis=0, concat_axis=0, tiled=True)
    sums = encode_far(odd, near[2], prepared)
    own, a, b = to_owners(sums, owned)
    staged = stage(mesh_latent, encoder_output, encoder_merge, encoder_self, process_sender)
    state, outgoing = merge(own, a, b, mesh_latent, asked, staged)
    r = receiver(grid_latent, decoder_receiver)
    src = edge_source[None, :]
    tgt = edge_target[None, :]
    for depth in range(LAYERS):
        last = depth == LAYERS - 1
        incoming = lax.all_to_all(
            outgoing.reshape(tiles, -1, 128),
            ("lat", "lon"),
            split_axis=0,
            concat_axis=0,
            tiled=True,
        ).reshape(outgoing.shape)
        prepared = ready(
            depth,
            last,
            state,
            tgt,
            process_receiver,
            process_self,
            process_output,
            process_merge,
            decoder_sender if last else process_sender,
        )
        result = layer(last, incoming, prepared, state, src, tgt, asked)
        if not last:
            state, outgoing = result
    near = neighbours(result[0])
    prepared = decode_near(odd, r, grid_latent, decoder_slots, near[:2], decoder_output)
    return decode_far(odd, near[2], prepared)


def solution(mesh):
    return jax.shard_map(
        body,
        mesh=mesh,
        in_specs=(
            P(("lat", "lon"), None),
            P(("lat", "lon"), None),
            P(None, ("lat", "lon")),
            P(None, ("lat", "lon")),
            P(("lat", "lon"), None, None),
            P(("lat", "lon")),
            P(("lat", "lon")),
            P(),
            P(),
            P(),
            P(),
            P(),
            P(),
            P(),
            P(),
            P(),
            P(),
            P(),
            P(),
            P(),
        ),
        out_specs=P(("lat", "lon"), None),
        check_vma=False,
    )
```

```python
import functools

import jax
import jax.numpy as jnp
from jax import lax
from jax.experimental import pallas as pl
from jax.experimental.pallas import tpu as pltpu
from jax.sharding import PartitionSpec as P


LAYERS = 2
ENC_FAN = 2
DEC_FAN = 3
SIDE = 3
ENC_ROWS = 1024
DEC_ROWS = 1024
FAR_ROWS = 1024
FAR_PART = 1024
PRE_ROWS = 1024


def up128(n):
    return -(-n // 128) * 128


def dot(left, right):
    return jnp.dot(left, right, preferred_element_type=jnp.float32)


def silu(v):
    half = 0.5 * v
    return half + half * jnp.tanh(half)


def silu_of_half(half):
    half = bf(half)
    return half + half * jnp.tanh(half)


def norm(v):
    centre = v - jnp.mean(v, axis=-1, keepdims=True)
    spread = jnp.mean(centre * centre, axis=-1, keepdims=True)
    return centre * lax.rsqrt(spread + 1e-05)


def hot_rows(row, width):
    n = row.shape[1]
    columns = jnp.broadcast_to(row, (128, n)).T
    lanes = lax.broadcasted_iota(jnp.int32, (n, 128), 1)
    parts = [
        jnp.where(lanes + at == columns, 1.0, 0.0).astype(jnp.bfloat16)
        for at in range(0, width, 128)
    ]
    return jnp.concatenate(parts, axis=1) if len(parts) > 1 else parts[0]


def hot_columns(row, height):
    subs = lax.broadcasted_iota(jnp.int32, (height, row.shape[1]), 0)
    return jnp.where(subs == row, 1.0, 0.0).astype(jnp.bfloat16)


def bf(v):
    return v.astype(jnp.bfloat16)


VMEM = pl.BlockSpec(memory_space=pltpu.VMEM)
HBM = pl.BlockSpec(memory_space=pltpu.HBM)


def near_to(space, arrays):
    return [pltpu.with_memory_space_constraint(x, space) for x in arrays]


def on_chip(kernel, args, outs, far=(), scratch=(), odd=None, limit=16):
    args = near_to(pltpu.VMEM, args)
    specs = [VMEM] * len(args) + [HBM] * len(far)
    args += near_to(pltpu.HBM, far)
    if odd is not None:
        args = [odd] + args
        specs = [pl.BlockSpec(memory_space=pltpu.SMEM)] + specs
    return pl.pallas_call(
        kernel,
        in_specs=specs,
        out_specs=[VMEM] * len(outs),
        out_shape=[pltpu.VMEM(shape, dtype) for shape, dtype in outs],
        scratch_shapes=list(scratch),
        compiler_params=pltpu.CompilerParams(vmem_limit_bytes=limit << 20),
    )(*args)


def fetch(pairs, sems):
    copies = [pltpu.make_async_copy(x, y, sems.at[i]) for i, (x, y) in enumerate(pairs)]
    for copy in copies:
        copy.start()
    return copies


def receiver_kernel(grid_ref, w_ref, r_ref):
    r_ref[...] = bf(dot(grid_ref[...], w_ref[...] * jnp.bfloat16(0.5)))


def receiver(grid_latent, w):
    n, d = grid_latent.shape
    tile = pl.BlockSpec((PRE_ROWS, d), lambda i: (i, 0))
    return pl.pallas_call(
        receiver_kernel,
        grid=(n // PRE_ROWS,),
        in_specs=[tile, pl.BlockSpec((d, d), lambda i: (0, 0))],
        out_specs=tile,
        out_shape=pltpu.HBM((n, d), jnp.bfloat16),
        compiler_params=pltpu.CompilerParams(vmem_limit_bytes=16 << 20),
        name="receiver",
    )(*near_to(pltpu.HBM, [grid_latent, w]))


def line_rows(rows, near, start, odd_ref):
    owned = rows.shape[0] // SIDE
    odd = odd_ref[1]
    for at, spot in enumerate((1, 2 - 2 * odd, 2 * odd)):
        to = pl.multiple_of(start + spot * owned, 16)
        near[pl.ds(to, owned), :] = rows[at * owned : (at + 1) * owned]


def line_start(place, odd_ref, line):
    odd = odd_ref[0]
    return (1, 2 - 2 * odd, 2 * odd)[place] * line


def up256(n):
    return -(-n // 256) * 256


def block_at(odd_ref, place):
    spots = []
    for axis, at in enumerate((place // SIDE, place % SIDE)):
        odd = odd_ref[axis]
        spots.append((1, 2 - 2 * odd, 2 * odd)[at])
    return spots[0] * SIDE + spots[1]


def enc_near_kernel(
    odd_ref, n0, n1, slots_ref, wr_ref, ws_ref, grid_ref, v_ref, slots, wr, near, ws, g, sems
):
    line = n0.shape[0]
    wide = near.shape[0] // 2
    rows = ENC_ROWS
    parts = [slice(i, i + rows) for i in range(0, g.shape[0], rows)]
    pairs = [(wr_ref, wr), (ws_ref, ws), (slots_ref, slots)]
    pairs += [(grid_ref.at[part], g.at[part]) for part in parts]
    copies = fetch(pairs, sems)
    near[...] = jnp.zeros_like(near)
    copies[0].wait()
    for k, ref in enumerate((n0, n1)):
        line_rows(bf(dot(ref[...], wr[...]) * 0.5), near, k * wide, odd_ref)
    copies[1].wait()
    copies[2].wait()
    for i, part in enumerate(parts):
        copies[3 + i].wait()
        s = dot(g[part], ws[...]) * 0.5
        for f in range(ENC_FAN):
            slot = slots[f : f + 1, part]
            chosen = jnp.concatenate(
                [hot_rows(slot - line_start(k, odd_ref, line), wide) for k in range(2)], axis=1
            )
            v_ref[f, part] = dot(chosen, near[...]) + s


def encode_near(odd, grid_latent, slot_rows, near, wr, ws):
    n, d = grid_latent.shape
    return on_chip(
        enc_near_kernel,
        list(near),
        [
            ((ENC_FAN, n, d), jnp.float32),
            (slot_rows.shape, jnp.int32),
            ((d, d), jnp.bfloat16),
        ],
        far=[slot_rows, wr, ws, grid_latent],
        scratch=[
            pltpu.VMEM((2 * up256(near[0].shape[0]), d), jnp.bfloat16),
            pltpu.VMEM((d, d), jnp.bfloat16),
            pltpu.VMEM((n, d), jnp.bfloat16),
            pltpu.SemaphoreType.DMA((3 + n // ENC_ROWS,)),
        ],
        odd=odd,
    )


def enc_far_kernel(odd_ref, n2, v_ref, slots_ref, wr_ref, o0, o1, o2, near, acc, hid):
    line = n2.shape[0]
    owned = line // SIDE
    slots = SIDE * line
    rows = hid.shape[0] // ENC_FAN

    near[...] = jnp.zeros_like(near)
    line_rows(bf(dot(n2[...], wr_ref[...]) * 0.5), near, 0, odd_ref)
    start = line_start(2, odd_ref, line)
    for step in range(v_ref.shape[1] // rows):
        part = slice(step * rows, (step + 1) * rows)
        for f in range(ENC_FAN):
            chosen = hot_rows(slots_ref[f : f + 1, part] - start, near.shape[0])
            v = dot(chosen, near[...]) + v_ref[f, part]
            hid[f * rows : (f + 1) * rows] = silu_of_half(v)
        chosen = jnp.concatenate(
            [hot_columns(slots_ref[f : f + 1, part], slots) for f in range(ENC_FAN)], axis=1
        )
        sums = dot(chosen, hid[...])
        acc[...] = sums if step == 0 else acc[...] + sums

    for k, ref in enumerate((o0, o1, o2)):
        for at in range(SIDE):
            first = pl.multiple_of(block_at(odd_ref, k * SIDE + at) * owned, 16)
            ref[at * owned : (at + 1) * owned] = bf(acc[pl.ds(first, owned), :])


def encode_far(odd, near, prepared):
    v, slots, wr = prepared
    line, d = near.shape
    return on_chip(
        enc_far_kernel,
        [near, v, slots, wr],
        [((line, d), jnp.bfloat16)] * SIDE,
        scratch=[
            pltpu.VMEM((up256(line), d), jnp.bfloat16),
            pltpu.VMEM((SIDE * line, d), jnp.float32),
            pltpu.VMEM((ENC_FAN * ENC_ROWS, d), jnp.bfloat16),
        ],
        odd=odd,
    )


def pack(sent, asked_ref, wide, out_ref):
    sent = padded_rows(bf(sent))
    tiles, cap = asked_ref.shape
    parts = sent.shape[1] // 128
    lanes = lax.broadcasted_iota(jnp.int32, (tiles, sent.shape[0]), 1)
    for k in range(cap):
        chosen = bf(jnp.where(lanes == asked_ref[:, k : k + 1], 1.0, 0.0))
        rows = dot(chosen, sent)
        for c in range(parts):
            wide[pl.ds(k * parts + c, tiles, stride=cap * parts), :] = rows[
                :, c * 128 : (c + 1) * 128
            ]
    out_ref[...] = bf(wide[...])


def unpack(in_ref, wide, d):
    parts = d // 128
    n = in_ref.shape[0] // parts
    wide[...] = in_ref[...].astype(jnp.float32)
    return jnp.concatenate(
        [bf(wide[pl.ds(c, n, stride=parts), :]) for c in range(parts)], axis=1
    )


def padded_rows(rows):
    extra = up128(rows.shape[0]) - rows.shape[0]
    return jnp.concatenate([rows, jnp.zeros((extra, rows.shape[1]), rows.dtype)], axis=0)


def stage_kernel(mesh, wo, wm, wself, ws, wom_out, ws_out, self_ref, w, sems):
    copies = fetch([(wself, w.at[0]), (wo, w.at[1]), (wm, w.at[2]), (ws.at[0], ws_out)], sems)
    copies[0].wait()
    self_ref[...] = dot(mesh[...], w[0])
    copies[1].wait()
    copies[2].wait()
    wom_out[...] = bf(dot(w[1], w[2]))
    copies[3].wait()


def stage(mesh, wo, wm, wself, ws):
    rows, d = mesh.shape
    return on_chip(
        stage_kernel,
        [mesh],
        [((d, d), jnp.bfloat16)] * 2 + [((rows, d), jnp.float32)],
        far=[wo, wm, wself, ws],
        scratch=[pltpu.VMEM((3, d, d), jnp.bfloat16), pltpu.SemaphoreType.DMA((4,))],
    )


def merge_kernel(
    o_ref, a_ref, b_ref, mesh_ref, asked_ref, wom, ws, self_ref, state_ref, out_ref, wide
):
    total = o_ref[...] + a_ref[...].astype(jnp.float32) + b_ref[...].astype(jnp.float32)
    update = dot(bf(total), wom[...]) + self_ref[...]
    state = bf(mesh_ref[...].astype(jnp.float32) + norm(silu(update)))
    state_ref[...] = state
    pack(dot(state, ws[...]), asked_ref, wide, out_ref)


def merge(own, a, b, mesh, asked, staged):
    packed = (asked.size * mesh.shape[1] // 128, 128)
    return on_chip(
        merge_kernel,
        [own, a, b, mesh, asked, *staged],
        [(mesh.shape, jnp.bfloat16), (packed, jnp.bfloat16)],
        scratch=[pltpu.VMEM(packed, jnp.float32)],
    )


def ready_kernel(
    depth, last, state_ref, tgt_ref, wr, wself, wo, wm, wn, base_ref, self_ref, wom, wn_out, w, sems
):
    pairs = [(x.at[depth], w.at[i]) for i, x in enumerate((wr, wself, wo, wm))]
    copies = fetch(pairs + [(wn if last else wn.at[depth + 1], wn_out)], sems)
    state = state_ref[...]
    chosen = hot_rows(tgt_ref[...], up128(state.shape[0]))
    copies[0].wait()
    received = padded_rows(bf(dot(state, w[0])))
    base_ref[...] = bf(dot(chosen, received))
    copies[1].wait()
    self_ref[...] = dot(state, w[1])
    copies[2].wait()
    copies[3].wait()
    wom[...] = bf(dot(w[2], w[3]))
    copies[4].wait()


def ready(depth, last, state, tgt, wr, wself, wo, wm, wn):
    rows, d = state.shape
    return on_chip(
        functools.partial(ready_kernel, depth, last),
        [state, tgt],
        [((tgt.shape[1], d), jnp.bfloat16), ((rows, d), jnp.float32)]
        + [((d, d), jnp.bfloat16)] * 2,
        far=[wr, wself, wo, wm, wn],
        scratch=[pltpu.VMEM((4, d, d), jnp.bfloat16), pltpu.SemaphoreType.DMA((5,))],
    )


def layer_kernel(
    last, in_ref, base_ref, self_ref, wom, wn, state_ref, src_ref, tgt_ref, asked_ref, *rest
):
    outs, wide = rest[:-1], rest[-1]
    owned, d = state_ref.shape
    incoming = unpack(in_ref, wide, d)
    v = dot(hot_rows(src_ref[...], incoming.shape[0]), incoming)
    hidden = bf(silu(v + base_ref[...].astype(jnp.float32)))
    gathered = dot(hot_columns(tgt_ref[...], owned), hidden)
    update = dot(bf(gathered), wom[...]) + self_ref[...]
    new = bf(state_ref[...].astype(jnp.float32) + norm(silu(update)))
    if last:
        outs[0][...] = bf(dot(new, wn[...]) * 0.5)
    else:
        outs[0][...] = new
        pack(dot(new, wn[...]), asked_ref, wide, outs[1])


def layer(last, incoming, prepared, state, src, tgt, asked):
    out = [(state.shape, jnp.bfloat16)]
    if not last:
        out.append((incoming.shape, jnp.bfloat16))
    return on_chip(
        functools.partial(layer_kernel, last),
        [incoming, *prepared, state, src, tgt, asked],
        out,
        scratch=[pltpu.VMEM(incoming.shape, jnp.float32)],
    )


def dec_near_kernel(
    odd_ref, n0, n1, slots_ref, wo_ref, grid_ref, r_ref, v_ref, slots, w, g, near, r, sems
):
    line = n0.shape[0]
    wide = near.shape[0] // 2
    rows = DEC_ROWS
    parts = [slice(i, i + rows) for i in range(0, r_ref.shape[0], rows)]
    pairs = [(slots_ref, slots)] + [(r_ref.at[part], r.at[part]) for part in parts]
    pairs += [(wo_ref, w), (grid_ref, g)]
    copies = fetch(pairs, sems)
    near[...] = jnp.zeros_like(near)
    for k, ref in enumerate((n0, n1)):
        line_rows(ref[...], near, k * wide, odd_ref)
    copies[0].wait()
    for i, part in enumerate(parts):
        copies[1 + i].wait()
        own = r[part].astype(jnp.float32)
        for f in range(DEC_FAN):
            slot = slots[f : f + 1, part]
            chosen = jnp.concatenate(
                [hot_rows(slot - line_start(k, odd_ref, line), wide) for k in range(2)], axis=1
            )
            v_ref[f, part] = dot(chosen, near[...]) + own
    for copy in copies[1 + len(parts) :]:
        copy.wait()


def dec_far_kernel(odd_ref, n2, v, slots, w, g, out_ref, near):
    line = n2.shape[0]
    rows = out_ref.shape[0]
    step = pl.program_id(0)

    @pl.when(step == 0)
    def _():
        near[...] = jnp.zeros_like(near)
        line_rows(n2[...], near, 0, odd_ref)

    start = line_start(2, odd_ref, line)
    for at in range(0, rows, FAR_PART):
        part = pl.ds(pl.multiple_of(step * rows + at, FAR_PART), FAR_PART)
        total = None
        for f in range(DEC_FAN):
            chosen = hot_rows(slots[f : f + 1, part] - start, near.shape[0])
            h = silu_of_half(dot(chosen, near[...]) + v[f, part, :]).astype(jnp.float32)
            total = h if total is None else total + h
        update = dot(bf(total), w[...])
        out_ref[at : at + FAR_PART] = bf(g[part, :].astype(jnp.float32) + norm(update))


def decode_near(odd, r, grid_latent, slot_rows, near, wo):
    n, d = r.shape
    wide = up256(near[0].shape[0])
    return on_chip(
        dec_near_kernel,
        list(near),
        [
            ((DEC_FAN, n, d), jnp.float32),
            (slot_rows.shape, jnp.int32),
            (wo.shape, jnp.bfloat16),
            ((n, d), jnp.bfloat16),
        ],
        far=[slot_rows, wo, grid_latent, r],
        scratch=[
            pltpu.VMEM((2 * wide, d), jnp.bfloat16),
            pltpu.VMEM((n, d), jnp.bfloat16),
            pltpu.SemaphoreType.DMA((3 + n // DEC_ROWS,)),
        ],
        odd=odd,
        limit=16,
    )


def decode_far(odd, near, prepared):
    v, slots, w, g = prepared
    n, d = g.shape
    args = near_to(pltpu.VMEM, [near, v, slots, w, g])
    return pl.pallas_call(
        dec_far_kernel,
        grid=(n // FAR_ROWS,),
        in_specs=[pl.BlockSpec(memory_space=pltpu.SMEM)] + [VMEM] * len(args),
        out_specs=pl.BlockSpec((FAR_ROWS, d), lambda i: (i, 0)),
        out_shape=jax.ShapeDtypeStruct((n, d), jnp.bfloat16),
        scratch_shapes=[pltpu.VMEM((up256(near.shape[0]), d), jnp.bfloat16)],
        compiler_params=pltpu.CompilerParams(vmem_limit_bytes=20 << 20),
        name="decode_far",
    )(odd, *args)


def swaps(axis):
    count = lax.axis_size(axis)
    first = [(i, i ^ 1) for i in range(count)]
    second = []
    for i in range(1, count - 1, 2):
        second += [(i, i + 1), (i + 1, i)]
    return first, second


def swap_both(axis, to_first, to_second):
    first, second = swaps(axis)
    b = lax.ppermute(to_second, axis, second)
    a = lax.ppermute(to_first, axis, first)
    return a, b


def neighbours(rows):
    a, b = swap_both("lon", rows, rows)
    line = jnp.concatenate([rows, a, b], axis=0)
    c, d = swap_both("lat", line, line)
    return line, c, d


def to_owners(sums, owned):
    a, b = swap_both("lat", sums[1], sums[2])

    def line(at):
        part = slice(at * owned, (at + 1) * owned)
        return (
            sums[0][part].astype(jnp.float32)
            + a[part].astype(jnp.float32)
            + b[part].astype(jnp.float32)
        )

    own, first, second = line(0), bf(line(1)), bf(line(2))
    c, d = swap_both("lon", first, second)
    return own, c, d


def body(
    grid_latent,
    mesh_latent,
    encoder_slots,
    decoder_slots,
    peer_rows,
    edge_source,
    edge_target,
    encoder_sender,
    encoder_receiver,
    encoder_output,
    encoder_merge,
    encoder_self,
    process_sender,
    process_receiver,
    process_output,
    process_merge,
    process_self,
    decoder_sender,
    decoder_receiver,
    decoder_output,
):
    owned = mesh_latent.shape[0]
    tiles = peer_rows.shape[1]
    odd = jnp.stack([lax.axis_index("lat") % 2, lax.axis_index("lon") % 2]).astype(jnp.int32)
    near = neighbours(mesh_latent)
    prepared = encode_near(
        odd, grid_latent, encoder_slots, near[:2], encoder_receiver, encoder_sender
    )
    wanted = jnp.maximum(peer_rows[0], 0)
    asked = lax.all_to_all(wanted, ("lat", "lon"), split_axis=0, concat_axis=0, tiled=True)
    sums = encode_far(odd, near[2], prepared)
    own, a, b = to_owners(sums, owned)
    staged = stage(mesh_latent, encoder_output, encoder_merge, encoder_self, process_sender)
    state, outgoing = merge(own, a, b, mesh_latent, asked, staged)
    r = receiver(grid_latent, decoder_receiver)
    src = edge_source[None, :]
    tgt = edge_target[None, :]
    for depth in range(LAYERS):
        last = depth == LAYERS - 1
        incoming = lax.all_to_all(
            outgoing.reshape(tiles, -1, 128),
            ("lat", "lon"),
            split_axis=0,
            concat_axis=0,
            tiled=True,
        ).reshape(outgoing.shape)
        prepared = ready(
            depth,
            last,
            state,
            tgt,
            process_receiver,
            process_self,
            process_output,
            process_merge,
            decoder_sender if last else process_sender,
        )
        result = layer(last, incoming, prepared, state, src, tgt, asked)
        if not last:
            state, outgoing = result
    near = neighbours(result[0])
    prepared = decode_near(odd, r, grid_latent, decoder_slots, near[:2], decoder_output)
    return decode_far(odd, near[2], prepared)


def solution(mesh):
    return jax.shard_map(
        body,
        mesh=mesh,
        in_specs=(
            P(("lat", "lon"), None),
            P(("lat", "lon"), None),
            P(None, ("lat", "lon")),
            P(None, ("lat", "lon")),
            P(("lat", "lon"), None, None),
            P(("lat", "lon")),
            P(("lat", "lon")),
            P(),
            P(),
            P(),
            P(),
            P(),
            P(),
            P(),
            P(),
            P(),
            P(),
            P(),
            P(),
            P(),
        ),
        out_specs=P(("lat", "lon"), None),
        check_vma=False,
    )
```

```python
import functools

import jax
import jax.numpy as jnp
from jax import lax
from jax.experimental import pallas as pl
from jax.experimental.pallas import tpu as pltpu
from jax.sharding import PartitionSpec as P


LAYERS = 2
ENC_FAN = 2
DEC_FAN = 3
SIDE = 3
ENC_ROWS = 1024
DEC_ROWS = 1024
FAR_ROWS = 1024
FAR_PART = 1024
PRE_ROWS = 1024


def up128(n):
    return -(-n // 128) * 128


def dot(left, right):
    return jnp.dot(left, right, preferred_element_type=jnp.float32)


def silu(v):
    half = 0.5 * v
    return half + half * jnp.tanh(half)


def silu_of_half(half):
    half = bf(half)
    return half + half * jnp.tanh(half)


def norm(v):
    centre = v - jnp.mean(v, axis=-1, keepdims=True)
    spread = jnp.mean(centre * centre, axis=-1, keepdims=True)
    return centre * lax.rsqrt(spread + 1e-05)


def hot_rows(row, width):
    n = row.shape[1]
    columns = jnp.broadcast_to(row, (128, n)).T
    lanes = lax.broadcasted_iota(jnp.int32, (n, 128), 1)
    parts = [
        jnp.where(lanes + at == columns, 1.0, 0.0).astype(jnp.bfloat16)
        for at in range(0, width, 128)
    ]
    return jnp.concatenate(parts, axis=1) if len(parts) > 1 else parts[0]


def hot_columns(row, height):
    subs = lax.broadcasted_iota(jnp.int32, (height, row.shape[1]), 0)
    return jnp.where(subs == row, 1.0, 0.0).astype(jnp.bfloat16)


def bf(v):
    return v.astype(jnp.bfloat16)


VMEM = pl.BlockSpec(memory_space=pltpu.VMEM)
HBM = pl.BlockSpec(memory_space=pltpu.HBM)


def near_to(space, arrays):
    return [pltpu.with_memory_space_constraint(x, space) for x in arrays]


def on_chip(kernel, args, outs, far=(), scratch=(), odd=None, limit=16):
    args = near_to(pltpu.VMEM, args)
    specs = [VMEM] * len(args) + [HBM] * len(far)
    args += near_to(pltpu.HBM, far)
    if odd is not None:
        args = [odd] + args
        specs = [pl.BlockSpec(memory_space=pltpu.SMEM)] + specs
    return pl.pallas_call(
        kernel,
        in_specs=specs,
        out_specs=[VMEM] * len(outs),
        out_shape=[pltpu.VMEM(shape, dtype) for shape, dtype in outs],
        scratch_shapes=list(scratch),
        compiler_params=pltpu.CompilerParams(vmem_limit_bytes=limit << 20),
    )(*args)


def fetch(pairs, sems):
    copies = [pltpu.make_async_copy(x, y, sems.at[i]) for i, (x, y) in enumerate(pairs)]
    for copy in copies:
        copy.start()
    return copies


def receiver_kernel(grid_ref, w_ref, r_ref):
    r_ref[...] = bf(dot(grid_ref[...], w_ref[...] * jnp.bfloat16(0.5)))


def receiver(grid_latent, w):
    n, d = grid_latent.shape
    tile = pl.BlockSpec((PRE_ROWS, d), lambda i: (i, 0))
    return pl.pallas_call(
        receiver_kernel,
        grid=(n // PRE_ROWS,),
        in_specs=[tile, pl.BlockSpec((d, d), lambda i: (0, 0))],
        out_specs=tile,
        out_shape=pltpu.HBM((n, d), jnp.bfloat16),
        compiler_params=pltpu.CompilerParams(vmem_limit_bytes=16 << 20),
        name="receiver",
    )(*near_to(pltpu.HBM, [grid_latent, w]))


def line_rows(rows, near, start, odd_ref):
    owned = rows.shape[0] // SIDE
    odd = odd_ref[1]
    for at, spot in enumerate((1, 2 - 2 * odd, 2 * odd)):
        to = pl.multiple_of(start + spot * owned, 16)
        near[pl.ds(to, owned), :] = rows[at * owned : (at + 1) * owned]


def line_start(place, odd_ref, line):
    odd = odd_ref[0]
    return (1, 2 - 2 * odd, 2 * odd)[place] * line


def up256(n):
    return -(-n // 256) * 256


def block_at(odd_ref, place):
    spots = []
    for axis, at in enumerate((place // SIDE, place % SIDE)):
        odd = odd_ref[axis]
        spots.append((1, 2 - 2 * odd, 2 * odd)[at])
    return spots[0] * SIDE + spots[1]


def enc_near_kernel(
    odd_ref, n0, n1, slots_ref, wr_ref, ws_ref, grid_ref, v_ref, slots, wr, near, ws, g, sems
):
    line = n0.shape[0]
    wide = near.shape[0] // 2
    rows = ENC_ROWS
    parts = [slice(i, i + rows) for i in range(0, g.shape[0], rows)]
    pairs = [(wr_ref, wr), (ws_ref, ws), (slots_ref, slots)]
    pairs += [(grid_ref.at[part], g.at[part]) for part in parts]
    copies = fetch(pairs, sems)
    near[...] = jnp.zeros_like(near)
    copies[0].wait()
    for k, ref in enumerate((n0, n1)):
        line_rows(bf(dot(ref[...], wr[...]) * 0.5), near, k * wide, odd_ref)
    copies[1].wait()
    copies[2].wait()
    for i, part in enumerate(parts):
        copies[3 + i].wait()
        s = dot(g[part], ws[...]) * 0.5
        for f in range(ENC_FAN):
            slot = slots[f : f + 1, part]
            chosen = jnp.concatenate(
                [hot_rows(slot - line_start(k, odd_ref, line), wide) for k in range(2)], axis=1
            )
            v_ref[f, part] = dot(chosen, near[...]) + s


def encode_near(odd, grid_latent, slot_rows, near, wr, ws):
    n, d = grid_latent.shape
    return on_chip(
        enc_near_kernel,
        list(near),
        [
            ((ENC_FAN, n, d), jnp.float32),
            (slot_rows.shape, jnp.int32),
            ((d, d), jnp.bfloat16),
        ],
        far=[slot_rows, wr, ws, grid_latent],
        scratch=[
            pltpu.VMEM((2 * up256(near[0].shape[0]), d), jnp.bfloat16),
            pltpu.VMEM((d, d), jnp.bfloat16),
            pltpu.VMEM((n, d), jnp.bfloat16),
            pltpu.SemaphoreType.DMA((3 + n // ENC_ROWS,)),
        ],
        odd=odd,
    )


def enc_far_kernel(odd_ref, n2, v_ref, slots_ref, wr_ref, o0, o1, o2, near, acc, hid):
    line = n2.shape[0]
    owned = line // SIDE
    slots = SIDE * line
    rows = hid.shape[0] // ENC_FAN

    near[...] = jnp.zeros_like(near)
    line_rows(bf(dot(n2[...], wr_ref[...]) * 0.5), near, 0, odd_ref)
    start = line_start(2, odd_ref, line)
    for step in range(v_ref.shape[1] // rows):
        part = slice(step * rows, (step + 1) * rows)
        for f in range(ENC_FAN):
            chosen = hot_rows(slots_ref[f : f + 1, part] - start, near.shape[0])
            v = dot(chosen, near[...]) + v_ref[f, part]
            hid[f * rows : (f + 1) * rows] = silu_of_half(v)
        chosen = jnp.concatenate(
            [hot_columns(slots_ref[f : f + 1, part], slots) for f in range(ENC_FAN)], axis=1
        )
        sums = dot(chosen, hid[...])
        acc[...] = sums if step == 0 else acc[...] + sums

    for k, ref in enumerate((o0, o1, o2)):
        for at in range(SIDE):
            first = pl.multiple_of(block_at(odd_ref, k * SIDE + at) * owned, 16)
            ref[at * owned : (at + 1) * owned] = bf(acc[pl.ds(first, owned), :])


def encode_far(odd, near, prepared):
    v, slots, wr = prepared
    line, d = near.shape
    return on_chip(
        enc_far_kernel,
        [near, v, slots, wr],
        [((line, d), jnp.bfloat16)] * SIDE,
        scratch=[
            pltpu.VMEM((up256(line), d), jnp.bfloat16),
            pltpu.VMEM((SIDE * line, d), jnp.float32),
            pltpu.VMEM((ENC_FAN * ENC_ROWS, d), jnp.bfloat16),
        ],
        odd=odd,
    )


def pack(sent, asked_ref, wide, out_ref):
    sent = padded_rows(bf(sent))
    tiles, cap = asked_ref.shape
    parts = sent.shape[1] // 128
    lanes = lax.broadcasted_iota(jnp.int32, (tiles, sent.shape[0]), 1)
    for k in range(cap):
        chosen = bf(jnp.where(lanes == asked_ref[:, k : k + 1], 1.0, 0.0))
        rows = dot(chosen, sent)
        for c in range(parts):
            wide[pl.ds(k * parts + c, tiles, stride=cap * parts), :] = rows[
                :, c * 128 : (c + 1) * 128
            ]
    out_ref[...] = bf(wide[...])


def unpack(in_ref, wide, d):
    parts = d // 128
    n = in_ref.shape[0] // parts
    wide[...] = in_ref[...].astype(jnp.float32)
    return jnp.concatenate(
        [bf(wide[pl.ds(c, n, stride=parts), :]) for c in range(parts)], axis=1
    )


def padded_rows(rows):
    extra = up128(rows.shape[0]) - rows.shape[0]
    return jnp.concatenate([rows, jnp.zeros((extra, rows.shape[1]), rows.dtype)], axis=0)


def stage_kernel(mesh, wo, wm, wself, ws, wom_out, ws_out, self_ref, w, sems):
    copies = fetch([(wself, w.at[0]), (wo, w.at[1]), (wm, w.at[2]), (ws.at[0], ws_out)], sems)
    copies[0].wait()
    self_ref[...] = dot(mesh[...], w[0])
    copies[1].wait()
    copies[2].wait()
    wom_out[...] = bf(dot(w[1], w[2]))
    copies[3].wait()


def stage(mesh, wo, wm, wself, ws):
    rows, d = mesh.shape
    return on_chip(
        stage_kernel,
        [mesh],
        [((d, d), jnp.bfloat16)] * 2 + [((rows, d), jnp.float32)],
        far=[wo, wm, wself, ws],
        scratch=[pltpu.VMEM((3, d, d), jnp.bfloat16), pltpu.SemaphoreType.DMA((4,))],
    )


def merge_kernel(
    o_ref, a_ref, b_ref, mesh_ref, asked_ref, wom, ws, self_ref, state_ref, out_ref, wide
):
    total = o_ref[...] + a_ref[...].astype(jnp.float32) + b_ref[...].astype(jnp.float32)
    update = dot(bf(total), wom[...]) + self_ref[...]
    state = bf(mesh_ref[...].astype(jnp.float32) + norm(silu(update)))
    state_ref[...] = state
    pack(dot(state, ws[...]), asked_ref, wide, out_ref)


def merge(own, a, b, mesh, asked, staged):
    packed = (asked.size * mesh.shape[1] // 128, 128)
    return on_chip(
        merge_kernel,
        [own, a, b, mesh, asked, *staged],
        [(mesh.shape, jnp.bfloat16), (packed, jnp.bfloat16)],
        scratch=[pltpu.VMEM(packed, jnp.float32)],
    )


def ready_kernel(
    depth, last, state_ref, tgt_ref, wr, wself, wo, wm, wn, base_ref, self_ref, wom, wn_out, w, sems
):
    pairs = [(x.at[depth], w.at[i]) for i, x in enumerate((wr, wself, wo, wm))]
    copies = fetch(pairs + [(wn if last else wn.at[depth + 1], wn_out)], sems)
    state = state_ref[...]
    chosen = hot_rows(tgt_ref[...], up128(state.shape[0]))
    copies[0].wait()
    received = padded_rows(bf(dot(state, w[0])))
    base_ref[...] = bf(dot(chosen, received))
    copies[1].wait()
    self_ref[...] = dot(state, w[1])
    copies[2].wait()
    copies[3].wait()
    wom[...] = bf(dot(w[2], w[3]))
    copies[4].wait()


def ready(depth, last, state, tgt, wr, wself, wo, wm, wn):
    rows, d = state.shape
    return on_chip(
        functools.partial(ready_kernel, depth, last),
        [state, tgt],
        [((tgt.shape[1], d), jnp.bfloat16), ((rows, d), jnp.float32)]
        + [((d, d), jnp.bfloat16)] * 2,
        far=[wr, wself, wo, wm, wn],
        scratch=[pltpu.VMEM((4, d, d), jnp.bfloat16), pltpu.SemaphoreType.DMA((5,))],
    )


def layer_kernel(
    last, in_ref, base_ref, self_ref, wom, wn, state_ref, src_ref, tgt_ref, asked_ref, *rest
):
    outs, wide = rest[:-1], rest[-1]
    owned, d = state_ref.shape
    incoming = unpack(in_ref, wide, d)
    v = dot(hot_rows(src_ref[...], incoming.shape[0]), incoming)
    hidden = bf(silu(v + base_ref[...].astype(jnp.float32)))
    gathered = dot(hot_columns(tgt_ref[...], owned), hidden)
    update = dot(bf(gathered), wom[...]) + self_ref[...]
    new = bf(state_ref[...].astype(jnp.float32) + norm(silu(update)))
    if last:
        outs[0][...] = bf(dot(new, wn[...]) * 0.5)
    else:
        outs[0][...] = new
        pack(dot(new, wn[...]), asked_ref, wide, outs[1])


def layer(last, incoming, prepared, state, src, tgt, asked):
    out = [(state.shape, jnp.bfloat16)]
    if not last:
        out.append((incoming.shape, jnp.bfloat16))
    return on_chip(
        functools.partial(layer_kernel, last),
        [incoming, *prepared, state, src, tgt, asked],
        out,
        scratch=[pltpu.VMEM(incoming.shape, jnp.float32)],
    )


def dec_near_kernel(
    odd_ref, n0, n1, slots_ref, wo_ref, grid_ref, r_ref, v_ref, slots, w, g, near, r, sems
):
    line = n0.shape[0]
    wide = near.shape[0] // 2
    rows = DEC_ROWS
    parts = [slice(i, i + rows) for i in range(0, r_ref.shape[0], rows)]
    pairs = [(slots_ref, slots)] + [(r_ref.at[part], r.at[part]) for part in parts]
    pairs += [(wo_ref, w), (grid_ref, g)]
    copies = fetch(pairs, sems)
    near[...] = jnp.zeros_like(near)
    for k, ref in enumerate((n0, n1)):
        line_rows(ref[...], near, k * wide, odd_ref)
    copies[0].wait()
    for i, part in enumerate(parts):
        copies[1 + i].wait()
        own = r[part].astype(jnp.float32)
        for f in range(DEC_FAN):
            slot = slots[f : f + 1, part]
            chosen = jnp.concatenate(
                [hot_rows(slot - line_start(k, odd_ref, line), wide) for k in range(2)], axis=1
            )
            v_ref[f, part] = dot(chosen, near[...]) + own
    for copy in copies[1 + len(parts) :]:
        copy.wait()


def dec_far_kernel(odd_ref, n2, v, slots, w, g, out_ref, near):
    line = n2.shape[0]
    rows = out_ref.shape[0]
    step = pl.program_id(0)

    @pl.when(step == 0)
    def _():
        near[...] = jnp.zeros_like(near)
        line_rows(n2[...], near, 0, odd_ref)

    start = line_start(2, odd_ref, line)
    for at in range(0, rows, FAR_PART):
        part = pl.ds(pl.multiple_of(step * rows + at, FAR_PART), FAR_PART)
        total = None
        chosen = jnp.concatenate(
            [hot_rows(slots[f : f + 1, part] - start, near.shape[0]) for f in range(DEC_FAN)], axis=0
        )
        most = dot(chosen, near[...])
        for f in range(DEC_FAN):
            h = silu_of_half(most[f * FAR_PART : (f + 1) * FAR_PART] + v[f, part, :])
            total = h if total is None else total + h
        update = dot(total, w[...])
        out_ref[at : at + FAR_PART] = bf(g[part, :].astype(jnp.float32) + norm(update))


def decode_near(odd, r, grid_latent, slot_rows, near, wo):
    n, d = r.shape
    wide = up256(near[0].shape[0])
    return on_chip(
        dec_near_kernel,
        list(near),
        [
            ((DEC_FAN, n, d), jnp.float32),
            (slot_rows.shape, jnp.int32),
            (wo.shape, jnp.bfloat16),
            ((n, d), jnp.bfloat16),
        ],
        far=[slot_rows, wo, grid_latent, r],
        scratch=[
            pltpu.VMEM((2 * wide, d), jnp.bfloat16),
            pltpu.VMEM((n, d), jnp.bfloat16),
            pltpu.SemaphoreType.DMA((3 + n // DEC_ROWS,)),
        ],
        odd=odd,
        limit=16,
    )


def decode_far(odd, near, prepared):
    v, slots, w, g = prepared
    n, d = g.shape
    args = near_to(pltpu.VMEM, [near, v, slots, w, g])
    return pl.pallas_call(
        dec_far_kernel,
        grid=(n // FAR_ROWS,),
        in_specs=[pl.BlockSpec(memory_space=pltpu.SMEM)] + [VMEM] * len(args),
        out_specs=pl.BlockSpec((FAR_ROWS, d), lambda i: (i, 0)),
        out_shape=jax.ShapeDtypeStruct((n, d), jnp.bfloat16),
        scratch_shapes=[pltpu.VMEM((up256(near.shape[0]), d), jnp.bfloat16)],
        compiler_params=pltpu.CompilerParams(vmem_limit_bytes=20 << 20),
        name="decode_far",
    )(odd, *args)


def swaps(axis):
    count = lax.axis_size(axis)
    first = [(i, i ^ 1) for i in range(count)]
    second = []
    for i in range(1, count - 1, 2):
        second += [(i, i + 1), (i + 1, i)]
    return first, second


def swap_both(axis, to_first, to_second):
    first, second = swaps(axis)
    b = lax.ppermute(to_second, axis, second)
    a = lax.ppermute(to_first, axis, first)
    return a, b


def neighbours(rows):
    a, b = swap_both("lon", rows, rows)
    line = jnp.concatenate([rows, a, b], axis=0)
    c, d = swap_both("lat", line, line)
    return line, c, d


def to_owners(sums, owned):
    a, b = swap_both("lat", sums[1], sums[2])

    def line(at):
        part = slice(at * owned, (at + 1) * owned)
        return (
            sums[0][part].astype(jnp.float32)
            + a[part].astype(jnp.float32)
            + b[part].astype(jnp.float32)
        )

    own, first, second = line(0), bf(line(1)), bf(line(2))
    c, d = swap_both("lon", first, second)
    return own, c, d


def body(
    grid_latent,
    mesh_latent,
    encoder_slots,
    decoder_slots,
    peer_rows,
    edge_source,
    edge_target,
    encoder_sender,
    encoder_receiver,
    encoder_output,
    encoder_merge,
    encoder_self,
    process_sender,
    process_receiver,
    process_output,
    process_merge,
    process_self,
    decoder_sender,
    decoder_receiver,
    decoder_output,
):
    owned = mesh_latent.shape[0]
    tiles = peer_rows.shape[1]
    odd = jnp.stack([lax.axis_index("lat") % 2, lax.axis_index("lon") % 2]).astype(jnp.int32)
    near = neighbours(mesh_latent)
    prepared = encode_near(
        odd, grid_latent, encoder_slots, near[:2], encoder_receiver, encoder_sender
    )
    wanted = jnp.maximum(peer_rows[0], 0)
    asked = lax.all_to_all(wanted, ("lat", "lon"), split_axis=0, concat_axis=0, tiled=True)
    sums = encode_far(odd, near[2], prepared)
    own, a, b = to_owners(sums, owned)
    staged = stage(mesh_latent, encoder_output, encoder_merge, encoder_self, process_sender)
    state, outgoing = merge(own, a, b, mesh_latent, asked, staged)
    r = receiver(grid_latent, decoder_receiver)
    src = edge_source[None, :]
    tgt = edge_target[None, :]
    for depth in range(LAYERS):
        last = depth == LAYERS - 1
        incoming = lax.all_to_all(
            outgoing.reshape(tiles, -1, 128),
            ("lat", "lon"),
            split_axis=0,
            concat_axis=0,
            tiled=True,
        ).reshape(outgoing.shape)
        prepared = ready(
            depth,
            last,
            state,
            tgt,
            process_receiver,
            process_self,
            process_output,
            process_merge,
            decoder_sender if last else process_sender,
        )
        result = layer(last, incoming, prepared, state, src, tgt, asked)
        if not last:
            state, outgoing = result
    near = neighbours(result[0])
    prepared = decode_near(odd, r, grid_latent, decoder_slots, near[:2], decoder_output)
    return decode_far(odd, near[2], prepared)


def solution(mesh):
    return jax.shard_map(
        body,
        mesh=mesh,
        in_specs=(
            P(("lat", "lon"), None),
            P(("lat", "lon"), None),
            P(None, ("lat", "lon")),
            P(None, ("lat", "lon")),
            P(("lat", "lon"), None, None),
            P(("lat", "lon")),
            P(("lat", "lon")),
            P(),
            P(),
            P(),
            P(),
            P(),
            P(),
            P(),
            P(),
            P(),
            P(),
            P(),
            P(),
            P(),
        ),
        out_specs=P(("lat", "lon"), None),
        check_vma=False,
    )
```

```python
import functools

import jax
import jax.numpy as jnp
from jax import lax
from jax.experimental import pallas as pl
from jax.experimental.pallas import tpu as pltpu
from jax.sharding import PartitionSpec as P


LAYERS = 2
ENC_FAN = 2
DEC_FAN = 3
SIDE = 3
ENC_ROWS = 1024
DEC_ROWS = 1024
OUT_ROWS = 512
FAR_PART = 1024
PRE_ROWS = 1024


def up128(n):
    return -(-n // 128) * 128


def dot(left, right):
    return jnp.dot(left, right, preferred_element_type=jnp.float32)


def silu(v):
    half = 0.5 * v
    return half + half * jnp.tanh(half)


def silu_of_half(half):
    half = bf(half)
    return half + half * jnp.tanh(half)


def norm(v):
    centre = v - jnp.mean(v, axis=-1, keepdims=True)
    spread = jnp.mean(centre * centre, axis=-1, keepdims=True)
    return centre * lax.rsqrt(spread + 1e-05)


def hot_rows(row, width):
    n = row.shape[1]
    columns = jnp.broadcast_to(row, (128, n)).T
    lanes = lax.broadcasted_iota(jnp.int32, (n, 128), 1)
    parts = [
        jnp.where(lanes + at == columns, 1.0, 0.0).astype(jnp.bfloat16)
        for at in range(0, width, 128)
    ]
    return jnp.concatenate(parts, axis=1) if len(parts) > 1 else parts[0]


def hot_columns(row, height):
    subs = lax.broadcasted_iota(jnp.int32, (height, row.shape[1]), 0)
    return jnp.where(subs == row, 1.0, 0.0).astype(jnp.bfloat16)


def bf(v):
    return v.astype(jnp.bfloat16)


VMEM = pl.BlockSpec(memory_space=pltpu.VMEM)
HBM = pl.BlockSpec(memory_space=pltpu.HBM)


def near_to(space, arrays):
    return [pltpu.with_memory_space_constraint(x, space) for x in arrays]


def on_chip(kernel, args, outs, far=(), scratch=(), odd=None, limit=16):
    args = near_to(pltpu.VMEM, args)
    specs = [VMEM] * len(args) + [HBM] * len(far)
    args += near_to(pltpu.HBM, far)
    if odd is not None:
        args = [odd] + args
        specs = [pl.BlockSpec(memory_space=pltpu.SMEM)] + specs
    return pl.pallas_call(
        kernel,
        in_specs=specs,
        out_specs=[VMEM] * len(outs),
        out_shape=[pltpu.VMEM(shape, dtype) for shape, dtype in outs],
        scratch_shapes=list(scratch),
        compiler_params=pltpu.CompilerParams(vmem_limit_bytes=limit << 20),
    )(*args)


def fetch(pairs, sems):
    copies = [pltpu.make_async_copy(x, y, sems.at[i]) for i, (x, y) in enumerate(pairs)]
    for copy in copies:
        copy.start()
    return copies


def receiver_kernel(grid_ref, w_ref, r_ref):
    r_ref[...] = bf(dot(grid_ref[...], w_ref[...] * jnp.bfloat16(0.5)))


def receiver(grid_latent, w):
    n, d = grid_latent.shape
    tile = pl.BlockSpec((PRE_ROWS, d), lambda i: (i, 0))
    return pl.pallas_call(
        receiver_kernel,
        grid=(n // PRE_ROWS,),
        in_specs=[tile, pl.BlockSpec((d, d), lambda i: (0, 0))],
        out_specs=tile,
        out_shape=pltpu.HBM((n, d), jnp.bfloat16),
        compiler_params=pltpu.CompilerParams(vmem_limit_bytes=16 << 20),
        name="receiver",
    )(*near_to(pltpu.HBM, [grid_latent, w]))


def line_rows(rows, near, start, odd_ref):
    owned = rows.shape[0] // SIDE
    odd = odd_ref[1]
    for at, spot in enumerate((1, 2 - 2 * odd, 2 * odd)):
        to = pl.multiple_of(start + spot * owned, 16)
        near[pl.ds(to, owned), :] = rows[at * owned : (at + 1) * owned]


def line_start(place, odd_ref, line):
    odd = odd_ref[0]
    return (1, 2 - 2 * odd, 2 * odd)[place] * line


def up256(n):
    return -(-n // 256) * 256


def block_at(odd_ref, place):
    spots = []
    for axis, at in enumerate((place // SIDE, place % SIDE)):
        odd = odd_ref[axis]
        spots.append((1, 2 - 2 * odd, 2 * odd)[at])
    return spots[0] * SIDE + spots[1]


def enc_near_kernel(
    odd_ref, n0, n1, slots_ref, wr_ref, ws_ref, grid_ref, v_ref, slots, wr, near, ws, g, sems
):
    line = n0.shape[0]
    wide = near.shape[0] // 2
    rows = ENC_ROWS
    parts = [slice(i, i + rows) for i in range(0, g.shape[0], rows)]
    pairs = [(wr_ref, wr), (ws_ref, ws), (slots_ref, slots)]
    pairs += [(grid_ref.at[part], g.at[part]) for part in parts]
    copies = fetch(pairs, sems)
    near[...] = jnp.zeros_like(near)
    copies[0].wait()
    for k, ref in enumerate((n0, n1)):
        line_rows(bf(dot(ref[...], wr[...]) * 0.5), near, k * wide, odd_ref)
    copies[1].wait()
    copies[2].wait()
    for i, part in enumerate(parts):
        copies[3 + i].wait()
        s = dot(g[part], ws[...]) * 0.5
        for f in range(ENC_FAN):
            slot = slots[f : f + 1, part]
            chosen = jnp.concatenate(
                [hot_rows(slot - line_start(k, odd_ref, line), wide) for k in range(2)], axis=1
            )
            v_ref[f, part] = dot(chosen, near[...]) + s


def encode_near(odd, grid_latent, slot_rows, near, wr, ws):
    n, d = grid_latent.shape
    return on_chip(
        enc_near_kernel,
        list(near),
        [
            ((ENC_FAN, n, d), jnp.float32),
            (slot_rows.shape, jnp.int32),
            ((d, d), jnp.bfloat16),
        ],
        far=[slot_rows, wr, ws, grid_latent],
        scratch=[
            pltpu.VMEM((2 * up256(near[0].shape[0]), d), jnp.bfloat16),
            pltpu.VMEM((d, d), jnp.bfloat16),
            pltpu.VMEM((n, d), jnp.bfloat16),
            pltpu.SemaphoreType.DMA((3 + n // ENC_ROWS,)),
        ],
        odd=odd,
    )


def enc_far_kernel(odd_ref, n2, v_ref, slots_ref, wr_ref, o0, o1, o2, near, acc, hid):
    line = n2.shape[0]
    owned = line // SIDE
    slots = SIDE * line
    rows = hid.shape[0] // ENC_FAN

    near[...] = jnp.zeros_like(near)
    line_rows(bf(dot(n2[...], wr_ref[...]) * 0.5), near, 0, odd_ref)
    start = line_start(2, odd_ref, line)
    for step in range(v_ref.shape[1] // rows):
        part = slice(step * rows, (step + 1) * rows)
        for f in range(ENC_FAN):
            chosen = hot_rows(slots_ref[f : f + 1, part] - start, near.shape[0])
            v = dot(chosen, near[...]) + v_ref[f, part]
            hid[f * rows : (f + 1) * rows] = silu_of_half(v)
        chosen = jnp.concatenate(
            [hot_columns(slots_ref[f : f + 1, part], slots) for f in range(ENC_FAN)], axis=1
        )
        sums = dot(chosen, hid[...])
        acc[...] = sums if step == 0 else acc[...] + sums

    for k, ref in enumerate((o0, o1, o2)):
        for at in range(SIDE):
            first = pl.multiple_of(block_at(odd_ref, k * SIDE + at) * owned, 16)
            ref[at * owned : (at + 1) * owned] = bf(acc[pl.ds(first, owned), :])


def encode_far(odd, near, prepared):
    v, slots, wr = prepared
    line, d = near.shape
    return on_chip(
        enc_far_kernel,
        [near, v, slots, wr],
        [((line, d), jnp.bfloat16)] * SIDE,
        scratch=[
            pltpu.VMEM((up256(line), d), jnp.bfloat16),
            pltpu.VMEM((SIDE * line, d), jnp.float32),
            pltpu.VMEM((ENC_FAN * ENC_ROWS, d), jnp.bfloat16),
        ],
        odd=odd,
    )


def pack(sent, asked_ref, wide, out_ref):
    sent = padded_rows(bf(sent))
    tiles, cap = asked_ref.shape
    parts = sent.shape[1] // 128
    lanes = lax.broadcasted_iota(jnp.int32, (tiles, sent.shape[0]), 1)
    for k in range(cap):
        chosen = bf(jnp.where(lanes == asked_ref[:, k : k + 1], 1.0, 0.0))
        rows = dot(chosen, sent)
        for c in range(parts):
            wide[pl.ds(k * parts + c, tiles, stride=cap * parts), :] = rows[
                :, c * 128 : (c + 1) * 128
            ]
    out_ref[...] = bf(wide[...])


def unpack(in_ref, wide, d):
    parts = d // 128
    n = in_ref.shape[0] // parts
    wide[...] = in_ref[...].astype(jnp.float32)
    return jnp.concatenate(
        [bf(wide[pl.ds(c, n, stride=parts), :]) for c in range(parts)], axis=1
    )


def padded_rows(rows):
    extra = up128(rows.shape[0]) - rows.shape[0]
    return jnp.concatenate([rows, jnp.zeros((extra, rows.shape[1]), rows.dtype)], axis=0)


def stage_kernel(mesh, wo, wm, wself, ws, wom_out, ws_out, self_ref, w, sems):
    copies = fetch([(wself, w.at[0]), (wo, w.at[1]), (wm, w.at[2]), (ws.at[0], ws_out)], sems)
    copies[0].wait()
    self_ref[...] = dot(mesh[...], w[0])
    copies[1].wait()
    copies[2].wait()
    wom_out[...] = bf(dot(w[1], w[2]))
    copies[3].wait()


def stage(mesh, wo, wm, wself, ws):
    rows, d = mesh.shape
    return on_chip(
        stage_kernel,
        [mesh],
        [((d, d), jnp.bfloat16)] * 2 + [((rows, d), jnp.float32)],
        far=[wo, wm, wself, ws],
        scratch=[pltpu.VMEM((3, d, d), jnp.bfloat16), pltpu.SemaphoreType.DMA((4,))],
    )


def merge_kernel(
    o_ref, a_ref, b_ref, mesh_ref, asked_ref, wom, ws, self_ref, state_ref, out_ref, wide
):
    total = o_ref[...] + a_ref[...].astype(jnp.float32) + b_ref[...].astype(jnp.float32)
    update = dot(bf(total), wom[...]) + self_ref[...]
    state = bf(mesh_ref[...].astype(jnp.float32) + norm(silu(update)))
    state_ref[...] = state
    pack(dot(state, ws[...]), asked_ref, wide, out_ref)


def merge(own, a, b, mesh, asked, staged):
    packed = (asked.size * mesh.shape[1] // 128, 128)
    return on_chip(
        merge_kernel,
        [own, a, b, mesh, asked, *staged],
        [(mesh.shape, jnp.bfloat16), (packed, jnp.bfloat16)],
        scratch=[pltpu.VMEM(packed, jnp.float32)],
    )


def ready_kernel(
    depth, last, state_ref, tgt_ref, wr, wself, wo, wm, wn, base_ref, self_ref, wom, wn_out, w, sems
):
    pairs = [(x.at[depth], w.at[i]) for i, x in enumerate((wr, wself, wo, wm))]
    copies = fetch(pairs + [(wn if last else wn.at[depth + 1], wn_out)], sems)
    state = state_ref[...]
    chosen = hot_rows(tgt_ref[...], up128(state.shape[0]))
    copies[0].wait()
    received = padded_rows(bf(dot(state, w[0])))
    base_ref[...] = bf(dot(chosen, received))
    copies[1].wait()
    self_ref[...] = dot(state, w[1])
    copies[2].wait()
    copies[3].wait()
    wom[...] = bf(dot(w[2], w[3]))
    copies[4].wait()


def ready(depth, last, state, tgt, wr, wself, wo, wm, wn):
    rows, d = state.shape
    return on_chip(
        functools.partial(ready_kernel, depth, last),
        [state, tgt],
        [((tgt.shape[1], d), jnp.bfloat16), ((rows, d), jnp.float32)]
        + [((d, d), jnp.bfloat16)] * 2,
        far=[wr, wself, wo, wm, wn],
        scratch=[pltpu.VMEM((4, d, d), jnp.bfloat16), pltpu.SemaphoreType.DMA((5,))],
    )


def layer_kernel(
    last, in_ref, base_ref, self_ref, wom, wn, state_ref, src_ref, tgt_ref, asked_ref, *rest
):
    outs, wide = rest[:-1], rest[-1]
    owned, d = state_ref.shape
    incoming = unpack(in_ref, wide, d)
    v = dot(hot_rows(src_ref[...], incoming.shape[0]), incoming)
    hidden = bf(silu(v + base_ref[...].astype(jnp.float32)))
    gathered = dot(hot_columns(tgt_ref[...], owned), hidden)
    update = dot(bf(gathered), wom[...]) + self_ref[...]
    new = bf(state_ref[...].astype(jnp.float32) + norm(silu(update)))
    if last:
        outs[0][...] = bf(dot(new, wn[...]) * 0.5)
    else:
        outs[0][...] = new
        pack(dot(new, wn[...]), asked_ref, wide, outs[1])


def layer(last, incoming, prepared, state, src, tgt, asked):
    out = [(state.shape, jnp.bfloat16)]
    if not last:
        out.append((incoming.shape, jnp.bfloat16))
    return on_chip(
        functools.partial(layer_kernel, last),
        [incoming, *prepared, state, src, tgt, asked],
        out,
        scratch=[pltpu.VMEM(incoming.shape, jnp.float32)],
    )


def dec_near_kernel(
    odd_ref, n0, n1, slots_ref, wo_ref, grid_ref, r_ref, v_ref, slots, w, g, near, r, sems
):
    line = n0.shape[0]
    wide = near.shape[0] // 2
    rows = DEC_ROWS
    parts = [slice(i, i + rows) for i in range(0, r_ref.shape[0], rows)]
    pairs = [(slots_ref, slots)] + [(r_ref.at[part], r.at[part]) for part in parts]
    pairs += [(wo_ref, w), (grid_ref, g)]
    copies = fetch(pairs, sems)
    near[...] = jnp.zeros_like(near)
    for k, ref in enumerate((n0, n1)):
        line_rows(ref[...], near, k * wide, odd_ref)
    copies[0].wait()
    for i, part in enumerate(parts):
        copies[1 + i].wait()
        own = r[part].astype(jnp.float32)
        for f in range(DEC_FAN):
            slot = slots[f : f + 1, part]
            chosen = jnp.concatenate(
                [hot_rows(slot - line_start(k, odd_ref, line), wide) for k in range(2)], axis=1
            )
            v_ref[f, part] = dot(chosen, near[...]) + own
    for copy in copies[1 + len(parts) :]:
        copy.wait()


def dec_far_kernel(odd_ref, n2, v, slots, w, g, out_ref, near, out, sems):
    line = n2.shape[0]
    rows = out_ref.shape[0]
    near[...] = jnp.zeros_like(near)
    line_rows(n2[...], near, 0, odd_ref)
    backs = []
    start = line_start(2, odd_ref, line)
    for at in range(0, rows, FAR_PART):
        part = pl.ds(at, FAR_PART)
        total = None
        chosen = jnp.concatenate(
            [hot_rows(slots[f : f + 1, part] - start, near.shape[0]) for f in range(DEC_FAN)], axis=0
        )
        most = dot(chosen, near[...])
        for f in range(DEC_FAN):
            h = silu_of_half(most[f * FAR_PART : (f + 1) * FAR_PART] + v[f, part, :])
            total = h if total is None else total + h
        update = dot(total, w[...])
        for k in range(0, FAR_PART, OUT_ROWS):
            to = slice(at + k, at + k + OUT_ROWS)
            out[to] = bf(g[to].astype(jnp.float32) + norm(update[k : k + OUT_ROWS]))
            backs.append(pltpu.make_async_copy(out.at[to], out_ref.at[to], sems.at[len(backs)]))
            backs[-1].start()
    for back in backs:
        back.wait()


def decode_near(odd, r, grid_latent, slot_rows, near, wo):
    n, d = r.shape
    wide = up256(near[0].shape[0])
    return on_chip(
        dec_near_kernel,
        list(near),
        [
            ((DEC_FAN, n, d), jnp.float32),
            (slot_rows.shape, jnp.int32),
            (wo.shape, jnp.bfloat16),
            ((n, d), jnp.bfloat16),
        ],
        far=[slot_rows, wo, grid_latent, r],
        scratch=[
            pltpu.VMEM((2 * wide, d), jnp.bfloat16),
            pltpu.VMEM((n, d), jnp.bfloat16),
            pltpu.SemaphoreType.DMA((3 + n // DEC_ROWS,)),
        ],
        odd=odd,
        limit=16,
    )


def decode_far(odd, near, prepared):
    v, slots, w, g = prepared
    n, d = g.shape
    args = near_to(pltpu.VMEM, [near, v, slots, w, g])
    return pl.pallas_call(
        dec_far_kernel,
        in_specs=[pl.BlockSpec(memory_space=pltpu.SMEM)] + [VMEM] * len(args),
        out_specs=HBM,
        out_shape=pltpu.HBM((n, d), jnp.bfloat16),
        scratch_shapes=[
            pltpu.VMEM((up256(near.shape[0]), d), jnp.bfloat16),
            pltpu.VMEM((n, d), jnp.bfloat16),
            pltpu.SemaphoreType.DMA((n // OUT_ROWS,)),
        ],
        compiler_params=pltpu.CompilerParams(vmem_limit_bytes=20 << 20),
        name="decode_far",
    )(odd, *args)


def swaps(axis):
    count = lax.axis_size(axis)
    first = [(i, i ^ 1) for i in range(count)]
    second = []
    for i in range(1, count - 1, 2):
        second += [(i, i + 1), (i + 1, i)]
    return first, second


def swap_both(axis, to_first, to_second):
    first, second = swaps(axis)
    b = lax.ppermute(to_second, axis, second)
    a = lax.ppermute(to_first, axis, first)
    return a, b


def neighbours(rows):
    a, b = swap_both("lon", rows, rows)
    line = jnp.concatenate([rows, a, b], axis=0)
    c, d = swap_both("lat", line, line)
    return line, c, d


def to_owners(sums, owned):
    a, b = swap_both("lat", sums[1], sums[2])

    def line(at):
        part = slice(at * owned, (at + 1) * owned)
        return (
            sums[0][part].astype(jnp.float32)
            + a[part].astype(jnp.float32)
            + b[part].astype(jnp.float32)
        )

    own, first, second = line(0), bf(line(1)), bf(line(2))
    c, d = swap_both("lon", first, second)
    return own, c, d


def body(
    grid_latent,
    mesh_latent,
    encoder_slots,
    decoder_slots,
    peer_rows,
    edge_source,
    edge_target,
    encoder_sender,
    encoder_receiver,
    encoder_output,
    encoder_merge,
    encoder_self,
    process_sender,
    process_receiver,
    process_output,
    process_merge,
    process_self,
    decoder_sender,
    decoder_receiver,
    decoder_output,
):
    owned = mesh_latent.shape[0]
    tiles = peer_rows.shape[1]
    odd = jnp.stack([lax.axis_index("lat") % 2, lax.axis_index("lon") % 2]).astype(jnp.int32)
    near = neighbours(mesh_latent)
    prepared = encode_near(
        odd, grid_latent, encoder_slots, near[:2], encoder_receiver, encoder_sender
    )
    wanted = jnp.maximum(peer_rows[0], 0)
    asked = lax.all_to_all(wanted, ("lat", "lon"), split_axis=0, concat_axis=0, tiled=True)
    sums = encode_far(odd, near[2], prepared)
    own, a, b = to_owners(sums, owned)
    staged = stage(mesh_latent, encoder_output, encoder_merge, encoder_self, process_sender)
    state, outgoing = merge(own, a, b, mesh_latent, asked, staged)
    r = receiver(grid_latent, decoder_receiver)
    src = edge_source[None, :]
    tgt = edge_target[None, :]
    for depth in range(LAYERS):
        last = depth == LAYERS - 1
        incoming = lax.all_to_all(
            outgoing.reshape(tiles, -1, 128),
            ("lat", "lon"),
            split_axis=0,
            concat_axis=0,
            tiled=True,
        ).reshape(outgoing.shape)
        prepared = ready(
            depth,
            last,
            state,
            tgt,
            process_receiver,
            process_self,
            process_output,
            process_merge,
            decoder_sender if last else process_sender,
        )
        result = layer(last, incoming, prepared, state, src, tgt, asked)
        if not last:
            state, outgoing = result
    near = neighbours(result[0])
    prepared = decode_near(odd, r, grid_latent, decoder_slots, near[:2], decoder_output)
    return decode_far(odd, near[2], prepared)


def solution(mesh):
    return jax.shard_map(
        body,
        mesh=mesh,
        in_specs=(
            P(("lat", "lon"), None),
            P(("lat", "lon"), None),
            P(None, ("lat", "lon")),
            P(None, ("lat", "lon")),
            P(("lat", "lon"), None, None),
            P(("lat", "lon")),
            P(("lat", "lon")),
            P(),
            P(),
            P(),
            P(),
            P(),
            P(),
            P(),
            P(),
            P(),
            P(),
            P(),
            P(),
            P(),
        ),
        out_specs=P(("lat", "lon"), None),
        check_vma=False,
    )
```
